32 devices in a mesh: dp: 4 (over y, x), ctx: 8 (over z, core).
Axes of the slice: x: 2, y: 2, z: 4, core: 2. Of those that a mesh axis runs over, the one named last changes fastest.
Arguments:
- tokens: bfloat16 [4, 1024, 1152], P('dp', 'ctx'), may hold values from -6 to 6
- starts: int32 [4, 4], P('dp'), may hold values from 0 to 768, as said below
- gain_attn: bfloat16 [1152], P('ctx'), may hold values from 0.099609375 to 1.8984375
- gain_mlp: bfloat16 [1152], P('ctx'), may hold values from 0.099609375 to 1.8984375
- w_query: bfloat16 [1152, 1152], P('ctx', 'dp'), may hold values from -0.1875 to 0.1875
- w_key: bfloat16 [1152, 384], P('ctx', 'dp'), may hold values from -0.1875 to 0.1875
- w_value: bfloat16 [1152, 384], P('ctx', 'dp'), may hold values from -0.1875 to 0.1875
- w_out: bfloat16 [1152, 1152], P('ctx', 'dp'), may hold values from -1.5 to 1.5
- w_gate: bfloat16 [1152, 3072], P('ctx', 'dp'), may hold values from -0.1875 to 0.1875
- w_up: bfloat16 [1152, 3072], P('ctx', 'dp'), may hold values from -0.1875 to 0.1875
- w_down: bfloat16 [3072, 1152], P('ctx', 'dp'), may hold values from -0.109375 to 0.109375
- cotangent: bfloat16 [4, 1024, 1152], P('dp', 'ctx'), may hold values from -6 to 6
Outputs:
- output: bfloat16 [4, 1024, 1152], P('dp', 'ctx')
- input_grad: float32 [4, 1024, 1152], P('dp', 'ctx')
- grad_gain_attn: float32 [1152], P('ctx')
- grad_gain_mlp: float32 [1152], P('ctx')
- grad_query: float32 [1152, 1152], P('ctx', 'dp')
- grad_key: float32 [1152, 384], P('ctx', 'dp')
- grad_value: float32 [1152, 384], P('ctx', 'dp')
- grad_out: float32 [1152, 1152], P('ctx', 'dp')
- grad_gate: float32 [1152, 3072], P('ctx', 'dp')
- grad_up: float32 [1152, 3072], P('ctx', 'dp')
- grad_down: float32 [3072, 1152], P('ctx', 'dp')
The draws below stay inside these ranges and needn't reach their ends.
Inputs may be any that keep to these rules, and one draw needn't show every extreme that they name: 4 pieces in each sequence, in increasing order; the p-th lies wholly within the p-th of 4 equal parts of the sequence; the first sequence's first piece starts at 0 and the last sequence's last piece ends at the sequence's end.
All inputs are finite; a program needn't handle non-finite values.
Results may differ from the reference program's by a relative error of at most 0.02.
Values may be sent and summed in bfloat16 or wider, within the bound.
A program may use at most 256 MiB of HBM per device.

```python
import jax
import jax.numpy as jnp
from jax import lax

D = 1152
HQ = 18
KEY_VALUE_HEADS = 6
HEAD_SIZE = 64
FF = 3072
TOK_DEV = 128
PIC = 256
PICS = 4
QW = 1152
KVW = 384
QUERY_PER_KV = 3
SEQUENCE_LENGTH = 1024
SEQS = 4
N_CTX = 8


def draw_starts(key, part):
    region = SEQUENCE_LENGTH // PICS
    offsets = jax.random.randint(key, (SEQS, PICS), 0, region - PIC + 1)
    rows = jnp.arange(SEQS).astype(jnp.int32)[:, None]
    cols = jnp.arange(PICS).astype(jnp.int32)[None, :]
    offsets = jnp.where((rows == 0) & (cols == 0), 0, offsets)
    offsets = jnp.where((rows == SEQS - 1) & (cols == PICS - 1), region - PIC, offsets)
    anchors = jnp.arange(PICS).astype(jnp.int32) * region
    return (anchors[None, :] + offsets).astype(jnp.int32)


def levels(own_key, extent, split, least, largest):
    def one(axis_at, blocks):
        draws = jax.random.uniform(jax.random.fold_in(jax.random.fold_in(own_key, 6), axis_at), (blocks,), jnp.float32, least / len(split), largest / len(split))
        return jnp.repeat(jnp.exp(draws), extent[axis_at] // blocks).reshape((-1,) + (1,) * (len(extent) - axis_at - 1))

    level = one(*split[0])
    for cut in split[1:]:
        level = level * one(*cut)
    return level


def normal_values(rng, shape, scale, limit, pieces=(), held_as=jnp.bfloat16):
    entries = scale * jax.random.normal(rng, shape, jnp.float32)
    if pieces:
        entries = entries * levels(rng, shape, pieces, -0.22, 0.18)
    return jnp.clip(entries, -limit, limit).astype(held_as)


def setup_inputs(seed: int = 0) -> dict:
    seeds = jax.random.split(jax.random.key(seed), 13)
    tokens = normal_values(seeds[0], (SEQS, SEQUENCE_LENGTH, D), 1.0, 6.0, ((0, 4), (1, 8)))
    starts = draw_starts(jax.random.fold_in(seeds[12], 71), 0)
    gain_attn = jnp.clip(1.0 + 0.18 * jax.random.normal(seeds[2], (D,), jnp.float32), 0.099609375, 1.8984375).astype(jnp.bfloat16)
    gain_mlp = jnp.clip(1.0 + 0.18 * jax.random.normal(seeds[3], (D,), jnp.float32), 0.099609375, 1.8984375).astype(jnp.bfloat16)
    w_query = normal_values(seeds[4], (D, QW), D ** -0.5, 0.1875, ((0, 8), (1, 4)))
    w_key = normal_values(seeds[5], (D, KVW), D ** -0.5, 0.1875, ((0, 8), (1, 4)))
    w_value = normal_values(seeds[6], (D, KVW), D ** -0.5, 0.1875, ((0, 8), (1, 4)))
    w_out = normal_values(seeds[7], (QW, D), (max(1, QW * 16 // (TOK_DEV * N_CTX))) ** -0.5, 1.5, ((0, 8), (1, 4)))
    w_gate = normal_values(seeds[8], (D, FF), D ** -0.5, 0.1875, ((0, 8), (1, 4)))
    w_up = normal_values(seeds[9], (D, FF), D ** -0.5, 0.1875, ((0, 8), (1, 4)))
    w_down = normal_values(seeds[10], (FF, D), FF ** -0.5, 0.109375, ((0, 8), (1, 4)))
    cotangent = normal_values(seeds[11], (SEQS, SEQUENCE_LENGTH, D), 1.0, 6.0, ((0, 4), (1, 8)))
    return dict(tokens=tokens, starts=starts, gain_attn=gain_attn, gain_mlp=gain_mlp, w_query=w_query, w_key=w_key, w_value=w_value, w_out=w_out, w_gate=w_gate, w_up=w_up, w_down=w_down, cotangent=cotangent)


norm_eps = 1e-05

@jax.custom_vjp
def low(v):
    return lax.optimization_barrier(v.astype(jnp.bfloat16)).astype(jnp.float32)

@jax.custom_vjp
def low_back(v):
    return v

def low_keep(v):
    return (low(v), None)

def low_pass(kept, grad):
    return (grad,)

def back_keep(v):
    return (v, None)

def back_low(kept, grad):
    return (low(grad),)
low.defvjp(low_keep, low_pass)
low_back.defvjp(back_keep, back_low)

def rotary_embedding(field, token_positions):
    half = field.shape[-1] // 2
    freqs = 10000.0 ** (-jnp.arange(half).astype(jnp.float32) / half)
    angles = token_positions.astype(jnp.float32)[:, None] * freqs[None, :]
    cosine = jnp.cos(angles)[:, None, :]
    sine = jnp.sin(angles)[:, None, :]
    first = field[..., :half]
    second = field[..., half:]
    return jnp.concatenate([first * cosine - second * sine, second * cosine + first * sine], axis=-1)

def piece_ids(token_positions, seq_starts):
    inside = (token_positions[:, None] >= seq_starts[None, :]) & (token_positions[:, None] < seq_starts[None, :] + PIC)
    labels = jnp.arange(1, PICS + 1).astype(jnp.int32)
    return (lax.optimization_barrier(jnp.sum(jnp.where(inside, labels[None, :], 0), axis=1)) - 1).astype(jnp.int32)

def matrix_product(left, right):
    return jnp.dot(left, right, precision=lax.Precision.HIGHEST)

def layer(stream, seq_starts, gain_one, gain_two, mat_query, key_projection, value_projection, mat_out, mat_gate, mat_up, mat_down):
    token_positions = jnp.arange(SEQUENCE_LENGTH).astype(jnp.int32)
    labels = piece_ids(token_positions, seq_starts)
    inv_one = lax.rsqrt(lax.optimization_barrier(jnp.mean(stream * stream, axis=-1, keepdims=True)) + norm_eps)
    attention_normed = low(stream * inv_one * gain_one)
    query_unrotated = low_back(matrix_product(attention_normed, mat_query)).reshape(SEQUENCE_LENGTH, HQ, HEAD_SIZE)
    key_unrotated = low_back(matrix_product(attention_normed, key_projection)).reshape(SEQUENCE_LENGTH, KEY_VALUE_HEADS, HEAD_SIZE)
    value_vectors = low(low_back(matrix_product(attention_normed, value_projection))).reshape(SEQUENCE_LENGTH, KEY_VALUE_HEADS, HEAD_SIZE)
    query_vectors = low(rotary_embedding(query_unrotated, token_positions)).reshape(SEQUENCE_LENGTH, KEY_VALUE_HEADS, QUERY_PER_KV, HEAD_SIZE)
    keys_all = low(rotary_embedding(key_unrotated, token_positions))
    span = min(512, SEQUENCE_LENGTH)
    score_scale = HEAD_SIZE ** (-0.5)

    def attend(block_index):
        first_row = block_index * span
        query_rows = lax.dynamic_slice_in_dim(query_vectors, first_row, span, 0)
        query_pos = first_row + jnp.arange(span).astype(jnp.int32)
        query_lab = lax.dynamic_slice_in_dim(labels, first_row, span, 0)
        scores = jnp.einsum('qhgd,khd->hgqk', query_rows, keys_all, precision=lax.Precision.HIGHEST) * score_scale
        scores = low_back(scores)
        allowed = (token_positions[None, :] <= query_pos[:, None]) | (query_lab[:, None] == labels[None, :]) & (query_lab[:, None] >= 0)
        scores = jnp.where(allowed[None, None], scores, -1e+30)
        biggest = lax.optimization_barrier(jnp.max(scores, axis=-1, keepdims=True))
        expo = jnp.exp(scores - biggest)
        probs = low(expo / lax.optimization_barrier(jnp.sum(expo, axis=-1, keepdims=True)))
        return jnp.einsum('hgqk,khd->qhgd', probs, value_vectors, precision=lax.Precision.HIGHEST)
    blocks = lax.map(jax.checkpoint(attend), jnp.arange(SEQUENCE_LENGTH // span).astype(jnp.int32))
    attended = low(low_back(blocks.reshape(SEQUENCE_LENGTH, HQ * HEAD_SIZE)))
    resid = stream + low_back(matrix_product(attended, mat_out))
    inv_two = lax.rsqrt(lax.optimization_barrier(jnp.mean(resid * resid, axis=-1, keepdims=True)) + norm_eps)
    normed_m = low(resid * inv_two * gain_two)
    gate_pre = low_back(matrix_product(normed_m, mat_gate))
    up_pre = low_back(matrix_product(normed_m, mat_up))
    hidden = low(jax.nn.silu(gate_pre) * up_pre)
    return resid + low_back(matrix_product(hidden, mat_down))

def reference(tokens, starts, gain_attn, gain_mlp, w_query, w_key, w_value, w_out, w_gate, w_up, w_down, cotangent):
    floats = tuple((item.astype(jnp.float32) for item in (tokens, gain_attn, gain_mlp, w_query, w_key, w_value, w_out, w_gate, w_up, w_down)))

    def forward(stream_all, gain_one, gain_two, mat_query, key_projection, value_projection, mat_out, mat_gate, mat_up, mat_down):

        def one_sequence(seq_stream, seq_starts):
            return layer(seq_stream, seq_starts, gain_one, gain_two, mat_query, key_projection, value_projection, mat_out, mat_gate, mat_up, mat_down)
        checked = jax.checkpoint(one_sequence)

        def step(running, pair):
            return (running, checked(pair[0], pair[1]))
        _, results = lax.scan(step, jnp.zeros((), jnp.float32), (stream_all, starts))
        return results
    result, pullback = jax.vjp(forward, *floats)
    grads = pullback(cotangent.astype(jnp.float32))
    return (result.astype(jnp.bfloat16), grads[0], grads[1], grads[2], grads[3], grads[4], grads[5], grads[6], grads[7], grads[8], grads[9])
```

```python
import jax
import jax.numpy as jnp
from jax import lax
from jax.sharding import PartitionSpec as P

HEAD_SIZE = 64
PIC = 256
PICS = 4


norm_eps = 1e-05


def rotary_embedding(field, token_positions):
    half = field.shape[-1] // 2
    freqs = 10000.0 ** (-jnp.arange(half).astype(jnp.float32) / half)
    angles = token_positions.astype(jnp.float32)[:, None] * freqs[None, :]
    cosine = jnp.cos(angles)[:, None, :]
    sine = jnp.sin(angles)[:, None, :]
    first = field[..., :half]
    second = field[..., half:]
    return jnp.concatenate(
        [first * cosine - second * sine, second * cosine + first * sine], axis=-1
    )


def rotary_back(field, token_positions):
    half = field.shape[-1] // 2
    freqs = 10000.0 ** (-jnp.arange(half).astype(jnp.float32) / half)
    angles = token_positions.astype(jnp.float32)[:, None] * freqs[None, :]
    cosine = jnp.cos(angles)[:, None, :]
    sine = jnp.sin(angles)[:, None, :]
    first = field[..., :half]
    second = field[..., half:]
    return jnp.concatenate(
        [first * cosine + second * sine, second * cosine - first * sine], axis=-1
    )


def piece_ids(token_positions, seq_starts):
    inside = (token_positions[:, None] >= seq_starts[None, :]) & (
        token_positions[:, None] < seq_starts[None, :] + PIC
    )
    labels = jnp.arange(1, PICS + 1)
    return jnp.sum(jnp.where(inside, labels[None, :], 0), axis=1) - 1


def norm_back(inputs, inverse, gain_vec, upstream):
    scaled = gain_vec * upstream
    return inverse * scaled - inputs * inverse**3 * jnp.mean(
        scaled * inputs, axis=-1, keepdims=True
    )


def fetch_weights(gain_attn, gain_mlp, w_query, w_key, w_value, w_out, w_gate, w_up, w_down):
    packed = jnp.concatenate([w_query, w_key, w_value, w_out], axis=1)
    gains = lax.all_gather(jnp.stack([gain_attn, gain_mlp]), "ctx", axis=1, tiled=True)
    packed = lax.all_gather(packed, ("dp", "ctx"), axis=0, tiled=True)
    packed = packed.reshape(lax.axis_size("dp"), -1, packed.shape[1])
    gate_up = lax.all_gather(jnp.concatenate([w_gate, w_up], axis=1), "ctx", axis=0, tiled=True)
    down = lax.all_gather(w_down, "ctx", axis=0, tiled=True)
    cuts = []
    first = 0
    for shard in (w_query, w_key, w_value, w_out):
        part = packed[:, :, first : first + shard.shape[1]]
        cuts.append(jnp.transpose(part, (1, 0, 2)).reshape(part.shape[1], -1))
        first += shard.shape[1]
    ff = w_gate.shape[1]
    return (gains[0], gains[1], *cuts, gate_up[:, :ff], gate_up[:, ff:], down)


def gather_keys(key_rot, value_low):
    return (
        lax.all_gather(key_rot, "ctx", axis=0, tiled=True),
        lax.all_gather(value_low, "ctx", axis=0, tiled=True),
    )


def delta_of(grad_rows, attended_rows):
    return jnp.transpose(jnp.sum(grad_rows.astype(jnp.float32) * attended_rows, axis=-1), (1, 2, 0))


def as_rows(stat):
    return jnp.transpose(stat, (2, 0, 1)).reshape(stat.shape[2], -1)


def body(
    tokens,
    starts,
    gain_attn,
    gain_mlp,
    w_query,
    w_key,
    w_value,
    w_out,
    w_gate,
    w_up,
    w_down,
    cotangent,
):
    tok_count = tokens.shape[1]
    length = tok_count * lax.axis_size("ctx")
    span = min(512, length)
    n_blocks = length // span
    query_pos = lax.axis_index("ctx") * tok_count + jnp.arange(tok_count)
    seq_starts = starts[0]
    labels_all = piece_ids(jnp.arange(length), seq_starts)

    def reach_of(token_positions):
        inside = (token_positions[:, None] >= seq_starts[None, :]) & (
            token_positions[:, None] < seq_starts[None, :] + PIC
        )
        return jnp.maximum(
            token_positions[-1], jnp.max(jnp.where(inside, seq_starts[None, :] + PIC - 1, -1))
        )

    gathered = fetch_weights(
        gain_attn, gain_mlp, w_query, w_key, w_value, w_out, w_gate, w_up, w_down
    )
    (
        gain_first,
        gain_second,
        mat_query,
        key_projection,
        value_projection,
        mat_out,
        mat_gate,
        mat_up,
        mat_down,
    ) = gathered
    heads_kv = key_projection.shape[1] // HEAD_SIZE
    group_size = mat_query.shape[1] // key_projection.shape[1]
    score_scale = HEAD_SIZE ** (-0.5)
    gain_one = gain_first.astype(jnp.float32)
    gain_two = gain_second.astype(jnp.float32)
    stream = tokens[0].astype(jnp.float32)
    inv_one = lax.rsqrt(jnp.mean(stream * stream, axis=-1, keepdims=True) + norm_eps)
    attention_normed = (stream * inv_one * gain_one).astype(jnp.bfloat16)
    query_unrotated = jnp.dot(attention_normed, mat_query, preferred_element_type=jnp.float32)
    key_unrotated = jnp.dot(attention_normed, key_projection, preferred_element_type=jnp.float32)
    v_pre = jnp.dot(attention_normed, value_projection, preferred_element_type=jnp.float32)
    query_vectors = (
        rotary_embedding(query_unrotated.reshape(tok_count, -1, HEAD_SIZE), query_pos)
        .astype(jnp.bfloat16)
        .reshape(tok_count, -1)
    )
    key_rot = (
        rotary_embedding(key_unrotated.reshape(tok_count, heads_kv, HEAD_SIZE), query_pos)
        .astype(jnp.bfloat16)
        .reshape(tok_count, -1)
    )
    value_low = v_pre.astype(jnp.bfloat16)
    key_all, value_all = gather_keys(key_rot, value_low)

    def key_block(source, block_index):
        return lax.dynamic_slice_in_dim(source, block_index * span, span, 0).reshape(
            span, heads_kv, HEAD_SIZE
        )

    def scores_at(block_index, key_piece, query_set, row_pos, row_lab):
        first_key = block_index * span
        key_pos = first_key + jnp.arange(span)
        key_lab = lax.dynamic_slice_in_dim(labels_all, first_key, span, 0)
        raw = (
            jnp.einsum("qhgd,khd->hgqk", query_set, key_piece, preferred_element_type=jnp.float32)
            * score_scale
        )
        allowed = (key_pos[None, :] <= row_pos[:, None]) | (
            row_lab[:, None] == key_lab[None, :]
        ) & (row_lab[:, None] >= 0)
        return jnp.where(allowed[None, None], raw, -1e30)

    keys_now = key_all
    values_now = value_all
    rows = query_vectors.shape[0]
    query_set = query_vectors.reshape(rows, heads_kv, group_size, HEAD_SIZE)
    row_lab = piece_ids(query_pos, seq_starts)
    reach = reach_of(query_pos)

    def lse_step(running, block_index):

        def lse_live(pair_now):
            most_now, sum_now = pair_now
            masked = scores_at(
                block_index, key_block(keys_now, block_index), query_set, query_pos, row_lab
            )
            most_new = jnp.maximum(most_now, jnp.max(masked, axis=-1))
            sum_new = sum_now * jnp.exp(most_now - most_new) + jnp.sum(
                jnp.exp(masked - most_new[..., None]), axis=-1
            )
            return (most_new, sum_new)

        return (
            lax.cond(block_index * span <= reach, lse_live, lambda pair_now: pair_now, running),
            None,
        )

    start_pair = (
        jnp.full((heads_kv, group_size, rows), -1e30, jnp.float32),
        jnp.zeros((heads_kv, group_size, rows), jnp.float32),
    )
    (most_all, sum_all), _ = lax.scan(lse_step, start_pair, jnp.arange(n_blocks))
    log_norm = most_all + jnp.log(sum_all)

    def out_step(running, block_index):

        def out_live(acc_now):
            masked = scores_at(
                block_index, key_block(keys_now, block_index), query_set, query_pos, row_lab
            )
            chances = jnp.exp(masked - log_norm[..., None]).astype(jnp.bfloat16)
            return acc_now + jnp.einsum(
                "hgqk,khd->qhgd",
                chances,
                key_block(values_now, block_index),
                preferred_element_type=jnp.float32,
            )

        return (
            lax.cond(block_index * span <= reach, out_live, lambda acc_now: acc_now, running),
            None,
        )

    attended_set, _ = lax.scan(
        out_step,
        jnp.zeros((rows, heads_kv, group_size, HEAD_SIZE), jnp.float32),
        jnp.arange(n_blocks),
    )
    att_low = attended_set.reshape(tok_count, -1).astype(jnp.bfloat16)
    resid = stream + jnp.dot(att_low, mat_out, preferred_element_type=jnp.float32)
    inv_two = lax.rsqrt(jnp.mean(resid * resid, axis=-1, keepdims=True) + norm_eps)
    normed_m = (resid * inv_two * gain_two).astype(jnp.bfloat16)
    width = mat_down.shape[1]
    group_normed = lax.all_gather(normed_m, "dp", axis=0, tiled=True)
    grad_low = cotangent[0]
    group_cot = lax.all_gather(grad_low, "dp", axis=0, tiled=True)
    cot_cols = lax.dynamic_slice_in_dim(group_cot, lax.axis_index("dp") * width, width, 1)
    grad_hidden_part = jnp.einsum(
        "td,fd->tf", cot_cols, mat_down, preferred_element_type=jnp.float32
    ).astype(jnp.bfloat16)
    grad_hidden = lax.psum_scatter(
        grad_hidden_part, "dp", scatter_dimension=1, tiled=True
    ).astype(jnp.float32)
    gate_pre = jnp.dot(group_normed, mat_gate, preferred_element_type=jnp.float32)
    up_pre = jnp.dot(group_normed, mat_up, preferred_element_type=jnp.float32)
    sigma = jax.nn.sigmoid(gate_pre)
    silu_val = gate_pre * sigma
    hidden = (silu_val * up_pre).astype(jnp.bfloat16)
    hidden_all = lax.all_gather(hidden, "dp", axis=1, tiled=True)
    down_cols = jnp.dot(hidden_all, mat_down, preferred_element_type=jnp.float32)
    down_rows = lax.all_to_all(
        down_cols.astype(jnp.bfloat16), "dp", split_axis=0, concat_axis=1, tiled=True
    )
    output = (resid + down_rows.astype(jnp.float32)).astype(jnp.bfloat16)
    grad_resid = grad_low.astype(jnp.float32)
    grad_down = jnp.einsum("tf,td->fd", hidden_all, cot_cols, preferred_element_type=jnp.float32)
    grad_gate_pre = (grad_hidden * up_pre * sigma * (1.0 + gate_pre * (1.0 - sigma))).astype(
        jnp.bfloat16
    )
    grad_up_pre = (grad_hidden * silu_val).astype(jnp.bfloat16)
    grad_gate = jnp.einsum(
        "td,tf->df", group_normed, grad_gate_pre, preferred_element_type=jnp.float32
    )
    grad_up = jnp.einsum(
        "td,tf->df", group_normed, grad_up_pre, preferred_element_type=jnp.float32
    )
    grad_nm = jnp.einsum("tf,df->td", grad_gate_pre, mat_gate, preferred_element_type=jnp.float32)
    grad_nm = grad_nm + jnp.einsum(
        "tf,df->td", grad_up_pre, mat_up, preferred_element_type=jnp.float32
    )
    grad_nm = lax.psum_scatter(
        grad_nm.astype(jnp.bfloat16), "dp", scatter_dimension=0, tiled=True
    ).astype(jnp.float32)
    grad_gain_two = jnp.sum(grad_nm * resid * inv_two, axis=0)
    grad_resid = grad_resid + norm_back(resid, inv_two, gain_two, grad_nm)
    grad_branch = grad_resid.astype(jnp.bfloat16)
    grad_wo = jnp.einsum("tq,td->qd", att_low, grad_branch, preferred_element_type=jnp.float32)
    grad_att = jnp.einsum(
        "td,qd->tq", grad_branch, mat_out, preferred_element_type=jnp.float32
    ).astype(jnp.bfloat16)
    delta_all = delta_of(grad_att.reshape(tok_count, heads_kv, group_size, HEAD_SIZE), attended_set)
    back_keys_now = key_all
    back_values_now = value_all
    rows = query_vectors.shape[0]
    back_query_set = query_vectors.reshape(rows, heads_kv, group_size, HEAD_SIZE)
    grad_set = grad_att.reshape(rows, heads_kv, group_size, HEAD_SIZE)
    back_row_lab = piece_ids(query_pos, seq_starts)
    back_reach = reach_of(query_pos)

    def back_step(running, block_index):

        def back_live(dq_acc):
            key_piece = key_block(back_keys_now, block_index)
            value_piece = key_block(back_values_now, block_index)
            masked = scores_at(block_index, key_piece, back_query_set, query_pos, back_row_lab)
            chances = jnp.exp(masked - log_norm[..., None])
            upstream = jnp.einsum(
                "qhgd,khd->hgqk", grad_set, value_piece, preferred_element_type=jnp.float32
            )
            score_grad = (chances * (upstream - delta_all[..., None])).astype(jnp.bfloat16)
            key_grad = score_scale * jnp.einsum(
                "hgqk,qhgd->khd", score_grad, back_query_set, preferred_element_type=jnp.float32
            )
            value_grad = jnp.einsum(
                "hgqk,qhgd->khd",
                chances.astype(jnp.bfloat16),
                grad_set,
                preferred_element_type=jnp.float32,
            )
            dq_new = dq_acc + score_scale * jnp.einsum(
                "hgqk,khd->qhgd", score_grad, key_piece, preferred_element_type=jnp.float32
            )
            return dq_new, (key_grad.astype(jnp.bfloat16), value_grad.astype(jnp.bfloat16))

        none_grad = jnp.zeros((span, heads_kv, HEAD_SIZE), jnp.bfloat16)
        return lax.cond(
            block_index * span <= back_reach,
            back_live,
            lambda dq_acc: (dq_acc, (none_grad, none_grad)),
            running,
        )

    dq_set, kv_parts = lax.scan(
        back_step,
        jnp.zeros((rows, heads_kv, group_size, HEAD_SIZE), jnp.float32),
        jnp.arange(n_blocks),
    )
    dq_low = (
        rotary_back(dq_set.reshape(rows, -1, HEAD_SIZE), query_pos)
        .reshape(rows, -1)
        .astype(jnp.bfloat16)
    )
    kv_parts = jnp.concatenate([part.reshape(length, -1) for part in kv_parts], axis=1)
    kv_sums = lax.psum_scatter(kv_parts, "ctx", scatter_dimension=0, tiled=True).astype(jnp.float32)
    key_grads = kv_sums[:, : heads_kv * HEAD_SIZE].reshape(tok_count, heads_kv, HEAD_SIZE)
    value_grads = kv_sums[:, heads_kv * HEAD_SIZE :]
    dk_low = rotary_back(key_grads, query_pos).reshape(tok_count, -1).astype(jnp.bfloat16)
    dv_low = value_grads.reshape(tok_count, -1).astype(jnp.bfloat16)
    grad_wq = jnp.einsum("td,tq->dq", attention_normed, dq_low, preferred_element_type=jnp.float32)
    grad_wk = jnp.einsum("td,tq->dq", attention_normed, dk_low, preferred_element_type=jnp.float32)
    grad_wv = jnp.einsum("td,tq->dq", attention_normed, dv_low, preferred_element_type=jnp.float32)
    grad_na = jnp.einsum("tq,dq->td", dq_low, mat_query, preferred_element_type=jnp.float32)
    grad_na = grad_na + jnp.einsum(
        "tq,dq->td", dk_low, key_projection, preferred_element_type=jnp.float32
    )
    grad_na = grad_na + jnp.einsum(
        "tq,dq->td", dv_low, value_projection, preferred_element_type=jnp.float32
    )
    grad_gain_one = jnp.sum(grad_na * stream * inv_one, axis=0)
    input_grad = grad_resid + norm_back(stream, inv_one, gain_one, grad_na)
    n_dp = lax.axis_size("dp")
    n_ctx = lax.axis_size("ctx")
    cut = jnp.concatenate(
        [
            jnp.transpose(
                part.astype(jnp.bfloat16).reshape(part.shape[0], n_dp, -1), (1, 0, 2)
            )
            for part in (grad_wq, grad_wk, grad_wv, grad_wo)
        ],
        axis=2,
    )
    mine = lax.psum_scatter(
        cut.reshape(-1, cut.shape[2]), ("dp", "ctx"), scatter_dimension=0, tiled=True
    ).astype(jnp.float32)
    gate_up_sum = lax.psum_scatter(
        jnp.concatenate([grad_gate, grad_up], axis=1).astype(jnp.bfloat16),
        "ctx",
        scatter_dimension=0,
        tiled=True,
    ).astype(jnp.float32)
    down_sum = lax.psum_scatter(
        grad_down.astype(jnp.bfloat16), "ctx", scatter_dimension=0, tiled=True
    ).astype(jnp.float32)
    ff = w_gate.shape[1]
    e_one = w_query.shape[1]
    e_two = e_one + w_key.shape[1]
    e_three = e_two + w_value.shape[1]
    shards = (
        mine[:, :e_one],
        mine[:, e_one:e_two],
        mine[:, e_two:e_three],
        mine[:, e_three:],
        gate_up_sum[:, :ff],
        gate_up_sum[:, ff:],
        down_sum,
    )
    gain_both = lax.psum(jnp.stack([grad_gain_one, grad_gain_two]), ("dp", "ctx"))
    gain_rows = gain_attn.shape[0]
    gain_sums = lax.dynamic_slice_in_dim(
        gain_both, lax.axis_index("ctx") * gain_rows, gain_rows, 1
    )
    return (
        output[None],
        input_grad[None],
        gain_sums[0],
        gain_sums[1],
        shards[0],
        shards[1],
        shards[2],
        shards[3],
        shards[4],
        shards[5],
        shards[6],
    )


def solution(mesh):
    return jax.shard_map(
        body,
        mesh=mesh,
        in_specs=(
            P("dp", "ctx", None),
            P("dp", None),
            P("ctx"),
            P("ctx"),
            P("ctx", "dp"),
            P("ctx", "dp"),
            P("ctx", "dp"),
            P("ctx", "dp"),
            P("ctx", "dp"),
            P("ctx", "dp"),
            P("ctx", "dp"),
            P("dp", "ctx", None),
        ),
        out_specs=(
            P("dp", "ctx", None),
            P("dp", "ctx", None),
            P("ctx"),
            P("ctx"),
            P("ctx", "dp"),
            P("ctx", "dp"),
            P("ctx", "dp"),
            P("ctx", "dp"),
            P("ctx", "dp"),
            P("ctx", "dp"),
            P("ctx", "dp"),
        ),
        check_vma=False,
    )
```

```python
import functools

import jax
import jax.numpy as jnp
from jax import lax
from jax.experimental import pallas as pl
from jax.experimental.pallas import tpu as pltpu
from jax.sharding import PartitionSpec as P

HEAD_SIZE = 64
PIC = 256
PICS = 4


norm_eps = 1e-05


def rotary_embedding(field, token_positions):
    half = field.shape[-1] // 2
    freqs = 10000.0 ** (-jnp.arange(half).astype(jnp.float32) / half)
    angles = token_positions.astype(jnp.float32)[:, None] * freqs[None, :]
    cosine = jnp.cos(angles)[:, None, :]
    sine = jnp.sin(angles)[:, None, :]
    first = field[..., :half]
    second = field[..., half:]
    return jnp.concatenate(
        [first * cosine - second * sine, second * cosine + first * sine], axis=-1
    )


def rotary_back(field, token_positions):
    half = field.shape[-1] // 2
    freqs = 10000.0 ** (-jnp.arange(half).astype(jnp.float32) / half)
    angles = token_positions.astype(jnp.float32)[:, None] * freqs[None, :]
    cosine = jnp.cos(angles)[:, None, :]
    sine = jnp.sin(angles)[:, None, :]
    first = field[..., :half]
    second = field[..., half:]
    return jnp.concatenate(
        [first * cosine + second * sine, second * cosine - first * sine], axis=-1
    )


def piece_ids(token_positions, seq_starts):
    inside = (token_positions[:, None] >= seq_starts[None, :]) & (
        token_positions[:, None] < seq_starts[None, :] + PIC
    )
    labels = jnp.arange(1, PICS + 1)
    return jnp.sum(jnp.where(inside, labels[None, :], 0), axis=1) - 1


def norm_back(inputs, inverse, gain_vec, upstream):
    scaled = gain_vec * upstream
    return inverse * scaled - inputs * inverse**3 * jnp.mean(
        scaled * inputs, axis=-1, keepdims=True
    )


def fetch_weights(gain_attn, gain_mlp, w_query, w_key, w_value, w_out, w_gate, w_up, w_down):
    packed = jnp.concatenate([w_query, w_key, w_value, w_out], axis=1)
    gains = lax.all_gather(jnp.stack([gain_attn, gain_mlp]), "ctx", axis=1, tiled=True)
    packed = lax.all_gather(packed, ("dp", "ctx"), axis=0, tiled=True)
    packed = packed.reshape(lax.axis_size("dp"), -1, packed.shape[1])
    gate_up = lax.all_gather(jnp.concatenate([w_gate, w_up], axis=1), "ctx", axis=0, tiled=True)
    down = lax.all_gather(w_down, "ctx", axis=0, tiled=True)
    cuts = []
    first = 0
    for shard in (w_query, w_key, w_value, w_out):
        part = packed[:, :, first : first + shard.shape[1]]
        cuts.append(jnp.transpose(part, (1, 0, 2)).reshape(part.shape[1], -1))
        first += shard.shape[1]
    ff = w_gate.shape[1]
    return (gains[0], gains[1], *cuts, gate_up[:, :ff], gate_up[:, ff:], down)


def gather_keys(key_rot, value_low):
    return (
        lax.all_gather(key_rot, "ctx", axis=0, tiled=True),
        lax.all_gather(value_low, "ctx", axis=0, tiled=True),
    )


def delta_of(grad_rows, attended_rows):
    return jnp.transpose(jnp.sum(grad_rows.astype(jnp.float32) * attended_rows, axis=-1), (1, 2, 0))


def as_rows(stat):
    return jnp.transpose(stat, (2, 0, 1)).reshape(stat.shape[2], -1)


def body(
    tokens,
    starts,
    gain_attn,
    gain_mlp,
    w_query,
    w_key,
    w_value,
    w_out,
    w_gate,
    w_up,
    w_down,
    cotangent,
):
    tok_count = tokens.shape[1]
    length = tok_count * lax.axis_size("ctx")
    span = min(512, length)
    n_blocks = length // span
    query_pos = lax.axis_index("ctx") * tok_count + jnp.arange(tok_count)
    seq_starts = starts[0]
    labels_all = piece_ids(jnp.arange(length), seq_starts)

    def reach_of(token_positions):
        inside = (token_positions[:, None] >= seq_starts[None, :]) & (
            token_positions[:, None] < seq_starts[None, :] + PIC
        )
        return jnp.maximum(
            token_positions[-1], jnp.max(jnp.where(inside, seq_starts[None, :] + PIC - 1, -1))
        )

    gathered = fetch_weights(
        gain_attn, gain_mlp, w_query, w_key, w_value, w_out, w_gate, w_up, w_down
    )
    (
        gain_first,
        gain_second,
        mat_query,
        key_projection,
        value_projection,
        mat_out,
        mat_gate,
        mat_up,
        mat_down,
    ) = gathered
    heads_kv = key_projection.shape[1] // HEAD_SIZE
    group_size = mat_query.shape[1] // key_projection.shape[1]
    score_scale = HEAD_SIZE ** (-0.5)
    gain_one = gain_first.astype(jnp.float32)
    gain_two = gain_second.astype(jnp.float32)
    stream = tokens[0].astype(jnp.float32)
    inv_one = lax.rsqrt(jnp.mean(stream * stream, axis=-1, keepdims=True) + norm_eps)
    attention_normed = (stream * inv_one * gain_one).astype(jnp.bfloat16)
    query_unrotated = jnp.dot(attention_normed, mat_query, preferred_element_type=jnp.float32)
    key_unrotated = jnp.dot(attention_normed, key_projection, preferred_element_type=jnp.float32)
    v_pre = jnp.dot(attention_normed, value_projection, preferred_element_type=jnp.float32)
    query_vectors = (
        rotary_embedding(query_unrotated.reshape(tok_count, -1, HEAD_SIZE), query_pos)
        .astype(jnp.bfloat16)
        .reshape(tok_count, -1)
    )
    key_rot = (
        rotary_embedding(key_unrotated.reshape(tok_count, heads_kv, HEAD_SIZE), query_pos)
        .astype(jnp.bfloat16)
        .reshape(tok_count, -1)
    )
    value_low = v_pre.astype(jnp.bfloat16)
    key_all, value_all = gather_keys(key_rot, value_low)

    def key_block(source, block_index):
        return lax.dynamic_slice_in_dim(source, block_index * span, span, 0).reshape(
            span, heads_kv, HEAD_SIZE
        )

    def scores_at(block_index, key_piece, query_set, row_pos, row_lab):
        first_key = block_index * span
        key_pos = first_key + jnp.arange(span)
        key_lab = lax.dynamic_slice_in_dim(labels_all, first_key, span, 0)
        raw = (
            jnp.einsum("qhgd,khd->hgqk", query_set, key_piece, preferred_element_type=jnp.float32)
            * score_scale
        )
        allowed = (key_pos[None, :] <= row_pos[:, None]) | (
            row_lab[:, None] == key_lab[None, :]
        ) & (row_lab[:, None] >= 0)
        return jnp.where(allowed[None, None], raw, -1e30)

    keys_now = key_all
    values_now = value_all
    rows = query_vectors.shape[0]
    query_set = query_vectors.reshape(rows, heads_kv, group_size, HEAD_SIZE)
    row_lab = piece_ids(query_pos, seq_starts)
    reach = reach_of(query_pos)

    def lse_step(running, block_index):

        def lse_live(pair_now):
            most_now, sum_now = pair_now
            masked = scores_at(
                block_index, key_block(keys_now, block_index), query_set, query_pos, row_lab
            )
            most_new = jnp.maximum(most_now, jnp.max(masked, axis=-1))
            sum_new = sum_now * jnp.exp(most_now - most_new) + jnp.sum(
                jnp.exp(masked - most_new[..., None]), axis=-1
            )
            return (most_new, sum_new)

        return (
            lax.cond(block_index * span <= reach, lse_live, lambda pair_now: pair_now, running),
            None,
        )

    start_pair = (
        jnp.full((heads_kv, group_size, rows), -1e30, jnp.float32),
        jnp.zeros((heads_kv, group_size, rows), jnp.float32),
    )
    (most_all, sum_all), _ = lax.scan(lse_step, start_pair, jnp.arange(n_blocks))
    log_norm = most_all + jnp.log(sum_all)

    def out_step(running, block_index):

        def out_live(acc_now):
            masked = scores_at(
                block_index, key_block(keys_now, block_index), query_set, query_pos, row_lab
            )
            chances = jnp.exp(masked - log_norm[..., None]).astype(jnp.bfloat16)
            return acc_now + jnp.einsum(
                "hgqk,khd->qhgd",
                chances,
                key_block(values_now, block_index),
                preferred_element_type=jnp.float32,
            )

        return (
            lax.cond(block_index * span <= reach, out_live, lambda acc_now: acc_now, running),
            None,
        )

    attended_set, _ = lax.scan(
        out_step,
        jnp.zeros((rows, heads_kv, group_size, HEAD_SIZE), jnp.float32),
        jnp.arange(n_blocks),
    )
    att_low = attended_set.reshape(tok_count, -1).astype(jnp.bfloat16)
    resid = stream + jnp.dot(att_low, mat_out, preferred_element_type=jnp.float32)
    inv_two = lax.rsqrt(jnp.mean(resid * resid, axis=-1, keepdims=True) + norm_eps)
    normed_m = (resid * inv_two * gain_two).astype(jnp.bfloat16)
    width = mat_down.shape[1]
    group_normed = lax.all_gather(normed_m, "dp", axis=0, tiled=True)
    grad_low = cotangent[0]
    group_cot = lax.all_gather(grad_low, "dp", axis=0, tiled=True)
    cot_cols = lax.dynamic_slice_in_dim(group_cot, lax.axis_index("dp") * width, width, 1)
    grad_hidden_part = jnp.einsum(
        "td,fd->tf", cot_cols, mat_down, preferred_element_type=jnp.float32
    ).astype(jnp.bfloat16)
    grad_hidden = lax.psum_scatter(
        grad_hidden_part, "dp", scatter_dimension=1, tiled=True
    ).astype(jnp.float32)
    gate_pre = jnp.dot(group_normed, mat_gate, preferred_element_type=jnp.float32)
    up_pre = jnp.dot(group_normed, mat_up, preferred_element_type=jnp.float32)
    sigma = jax.nn.sigmoid(gate_pre)
    silu_val = gate_pre * sigma
    hidden = (silu_val * up_pre).astype(jnp.bfloat16)
    hidden_all = lax.all_gather(hidden, "dp", axis=1, tiled=True)
    down_cols = jnp.dot(hidden_all, mat_down, preferred_element_type=jnp.float32)
    down_rows = lax.all_to_all(
        down_cols.astype(jnp.bfloat16), "dp", split_axis=0, concat_axis=1, tiled=True
    )
    output = (resid + down_rows.astype(jnp.float32)).astype(jnp.bfloat16)
    grad_resid = grad_low.astype(jnp.float32)
    grad_down = jnp.einsum("tf,td->fd", hidden_all, cot_cols, preferred_element_type=jnp.float32)
    grad_gate_pre = (grad_hidden * up_pre * sigma * (1.0 + gate_pre * (1.0 - sigma))).astype(
        jnp.bfloat16
    )
    grad_up_pre = (grad_hidden * silu_val).astype(jnp.bfloat16)
    grad_gate = jnp.einsum(
        "td,tf->df", group_normed, grad_gate_pre, preferred_element_type=jnp.float32
    )
    grad_up = jnp.einsum(
        "td,tf->df", group_normed, grad_up_pre, preferred_element_type=jnp.float32
    )
    grad_nm = jnp.einsum("tf,df->td", grad_gate_pre, mat_gate, preferred_element_type=jnp.float32)
    grad_nm = grad_nm + jnp.einsum(
        "tf,df->td", grad_up_pre, mat_up, preferred_element_type=jnp.float32
    )
    grad_nm = lax.psum_scatter(
        grad_nm.astype(jnp.bfloat16), "dp", scatter_dimension=0, tiled=True
    ).astype(jnp.float32)
    grad_gain_two = jnp.sum(grad_nm * resid * inv_two, axis=0)
    grad_resid = grad_resid + norm_back(resid, inv_two, gain_two, grad_nm)
    grad_branch = grad_resid.astype(jnp.bfloat16)
    grad_wo = jnp.einsum("tq,td->qd", att_low, grad_branch, preferred_element_type=jnp.float32)
    grad_att = jnp.einsum(
        "td,qd->tq", grad_branch, mat_out, preferred_element_type=jnp.float32
    ).astype(jnp.bfloat16)
    delta_all = delta_of(grad_att.reshape(tok_count, heads_kv, group_size, HEAD_SIZE), attended_set)
    back_keys_now = key_all
    back_values_now = value_all
    rows = query_vectors.shape[0]
    back_query_set = query_vectors.reshape(rows, heads_kv, group_size, HEAD_SIZE)
    grad_set = grad_att.reshape(rows, heads_kv, group_size, HEAD_SIZE)
    back_row_lab = piece_ids(query_pos, seq_starts)
    back_reach = reach_of(query_pos)

    def back_step(running, block_index):

        def back_live(dq_acc):
            key_piece = key_block(back_keys_now, block_index)
            value_piece = key_block(back_values_now, block_index)
            masked = scores_at(block_index, key_piece, back_query_set, query_pos, back_row_lab)
            chances = jnp.exp(masked - log_norm[..., None])
            upstream = jnp.einsum(
                "qhgd,khd->hgqk", grad_set, value_piece, preferred_element_type=jnp.float32
            )
            score_grad = (chances * (upstream - delta_all[..., None])).astype(jnp.bfloat16)
            key_grad = score_scale * jnp.einsum(
                "hgqk,qhgd->khd", score_grad, back_query_set, preferred_element_type=jnp.float32
            )
            value_grad = jnp.einsum(
                "hgqk,qhgd->khd",
                chances.astype(jnp.bfloat16),
                grad_set,
                preferred_element_type=jnp.float32,
            )
            dq_new = dq_acc + score_scale * jnp.einsum(
                "hgqk,khd->qhgd", score_grad, key_piece, preferred_element_type=jnp.float32
            )
            return dq_new, (key_grad.astype(jnp.bfloat16), value_grad.astype(jnp.bfloat16))

        none_grad = jnp.zeros((span, heads_kv, HEAD_SIZE), jnp.bfloat16)
        return lax.cond(
            block_index * span <= back_reach,
            back_live,
            lambda dq_acc: (dq_acc, (none_grad, none_grad)),
            running,
        )

    dq_set, kv_parts = lax.scan(
        back_step,
        jnp.zeros((rows, heads_kv, group_size, HEAD_SIZE), jnp.float32),
        jnp.arange(n_blocks),
    )
    dq_low = (
        rotary_back(dq_set.reshape(rows, -1, HEAD_SIZE), query_pos)
        .reshape(rows, -1)
        .astype(jnp.bfloat16)
    )
    kv_parts = jnp.concatenate([part.reshape(length, -1) for part in kv_parts], axis=1)
    kv_sums = lax.psum_scatter(kv_parts, "ctx", scatter_dimension=0, tiled=True).astype(jnp.float32)
    key_grads = kv_sums[:, : heads_kv * HEAD_SIZE].reshape(tok_count, heads_kv, HEAD_SIZE)
    value_grads = kv_sums[:, heads_kv * HEAD_SIZE :]
    dk_low = rotary_back(key_grads, query_pos).reshape(tok_count, -1).astype(jnp.bfloat16)
    dv_low = value_grads.reshape(tok_count, -1).astype(jnp.bfloat16)
    grad_wq = jnp.einsum("td,tq->dq", attention_normed, dq_low, preferred_element_type=jnp.float32)
    grad_wk = jnp.einsum("td,tq->dq", attention_normed, dk_low, preferred_element_type=jnp.float32)
    grad_wv = jnp.einsum("td,tq->dq", attention_normed, dv_low, preferred_element_type=jnp.float32)
    grad_na = jnp.einsum("tq,dq->td", dq_low, mat_query, preferred_element_type=jnp.float32)
    grad_na = grad_na + jnp.einsum(
        "tq,dq->td", dk_low, key_projection, preferred_element_type=jnp.float32
    )
    grad_na = grad_na + jnp.einsum(
        "tq,dq->td", dv_low, value_projection, preferred_element_type=jnp.float32
    )
    grad_gain_one = jnp.sum(grad_na * stream * inv_one, axis=0)
    input_grad = grad_resid + norm_back(stream, inv_one, gain_one, grad_na)
    n_dp = lax.axis_size("dp")
    n_ctx = lax.axis_size("ctx")
    cut = jnp.concatenate(
        [
            jnp.transpose(
                part.astype(jnp.bfloat16).reshape(part.shape[0], n_dp, -1), (1, 0, 2)
            )
            for part in (grad_wq, grad_wk, grad_wv, grad_wo)
        ],
        axis=2,
    )
    mine = lax.psum_scatter(
        cut.reshape(-1, cut.shape[2]), ("dp", "ctx"), scatter_dimension=0, tiled=True
    ).astype(jnp.float32)
    gate_up_sum = lax.psum_scatter(
        jnp.concatenate([grad_gate, grad_up], axis=1).astype(jnp.bfloat16),
        "ctx",
        scatter_dimension=0,
        tiled=True,
    ).astype(jnp.float32)
    down_sum = lax.psum_scatter(
        grad_down.astype(jnp.bfloat16), "ctx", scatter_dimension=0, tiled=True
    ).astype(jnp.float32)
    ff = w_gate.shape[1]
    e_one = w_query.shape[1]
    e_two = e_one + w_key.shape[1]
    e_three = e_two + w_value.shape[1]
    shards = (
        mine[:, :e_one],
        mine[:, e_one:e_two],
        mine[:, e_two:e_three],
        mine[:, e_three:],
        gate_up_sum[:, :ff],
        gate_up_sum[:, ff:],
        down_sum,
    )
    gain_both = lax.psum(jnp.stack([grad_gain_one, grad_gain_two]), ("dp", "ctx"))
    gain_rows = gain_attn.shape[0]
    gain_sums = lax.dynamic_slice_in_dim(
        gain_both, lax.axis_index("ctx") * gain_rows, gain_rows, 1
    )
    return (
        output[None],
        input_grad[None],
        gain_sums[0],
        gain_sums[1],
        shards[0],
        shards[1],
        shards[2],
        shards[3],
        shards[4],
        shards[5],
        shards[6],
    )


BF = jnp.bfloat16
F32 = jnp.float32
MESH = pl.DeviceIdType.MESH


def dot_nn(left, right):
    return lax.dot_general(left, right, (((1,), (0,)), ((), ())), preferred_element_type=F32)


def dot_nt(left, right):
    return lax.dot_general(left, right, (((1,), (1,)), ((), ())), preferred_element_type=F32)


def shift_lanes(field, amount):
    return pltpu.roll(field, amount, 1)


def widen(field, lanes):
    return jnp.concatenate(
        [field, jnp.zeros((field.shape[0], lanes - field.shape[1]), field.dtype)], axis=1
    )


def fast_kernel(
    n_dp,
    n_ctx,
    tok,
    cot,
    starts,
    gains,
    cos_ref,
    sin_ref,
    w_pack,
    w_gate,
    w_up,
    w_down,
    out_ref,
    ig_ref,
    gg_ref,
    g_pack_ref,
    g_gu_ref,
    g_down_ref,
    gb,
    wt,
    big,
    wd,
    na_ref,
    qt,
    kvb,
    sc,
    pp,
    rl,
    at,
    resid_ref,
    xb,
    cb,
    op,
    orecv,
    dn,
    drecv,
    dna,
    hb,
    dgu,
    xt,
    ht,
    gres,
    dat,
    rb,
    dkv,
    dkv_r,
    dkv_z,
    kvsum,
    gu_r,
    gu_z,
    gd,
    gd_r,
    gd_z,
    g_r,
    g_p,
    g_z,
    nat,
    ggs,
    gg_p,
    gg_c,
    s_send,
    s_gain,
    s_a,
    s_ap,
    s_b,
    s_bz,
    s_bp,
    s_kv,
    s_gu,
    s_wd,
    s_x,
    s_c,
    s_o,
    s_d,
    s_dkv,
    s_gur,
    s_gdr,
    s_gdz,
    s_gr,
    s_gp,
    s_gz,
    s_ggp,
    s_ggc,
):
    n_z = n_ctx // 2
    rows_tok, model = tok.shape
    shard_rows = w_pack.shape[0]
    cq = model // n_dp
    ck = 96
    ffs = w_gate.shape[1]
    rf = w_down.shape[0]
    kvh = 6
    group = 3
    hs = HEAD_SIZE
    gl = group * rows_tok
    pack = w_pack.shape[1]
    d = lax.axis_index("dp")
    c = lax.axis_index("ctx")
    k = lax.rem(c, 2)
    z = c // 2
    mate = c + 1 - 2 * k
    my_down = pl.multiple_of(k * rf, 128)
    its_down = pl.multiple_of((1 - k) * rf, 128)
    pending = []
    counter = [0]

    def zc(i):
        return 2 * lax.rem(z + i, n_z) + k

    def dd_of(i):
        return lax.rem(d + i, n_dp)

    def rdma(src, dst, rsem, to_d, to_c):
        ssem = s_send.at[counter[0]]
        counter[0] += 1
        copy = pltpu.make_async_remote_copy(
            src_ref=src,
            dst_ref=dst,
            send_sem=ssem,
            recv_sem=rsem,
            device_id=(to_d, to_c),
            device_id_type=MESH,
        )
        copy.start()
        pending.append(copy)
        return copy

    def arrived(dst, rsem):
        pltpu.make_async_remote_copy(
            src_ref=dst,
            dst_ref=dst,
            send_sem=s_send.at[0],
            recv_sem=rsem,
            device_id=(d, mate),
            device_id_type=MESH,
        ).wait_recv()

    wt[d, z, k] = w_pack[...]
    gb[c] = gains[...]
    la = pl.ds(0, 512)
    lb = pl.ds(512, pack - 512)
    for i in range(1, n_z):
        rdma(wt.at[d, z, k, :, la], wt.at[d, z, k, :, la], s_a.at[0, n_z - i], d, zc(i))
    for i in range(1, n_dp):
        rdma(wt.at[d, z, k, :, la], wt.at[d, z, k, :, la], s_a.at[n_dp - i, 0], dd_of(i), c)
    for i in range(1, n_ctx):
        rdma(gb.at[c], gb.at[c], s_gain.at[n_ctx - i], d, lax.rem(c + i, n_ctx))
    big[k, 0, z] = w_gate[...]
    big[k, 1, z] = w_up[...]
    own = n_dp - 1
    cot_v = cot[...].astype(F32)
    for e in range(n_dp):
        turned = cot_v if e == 0 else shift_lanes(cot_v, model - cq * e)
        cb[own, e] = turned[:, :384].astype(BF)
    stream = tok[...].astype(F32)
    inv1 = lax.rsqrt(jnp.mean(stream * stream, axis=1, keepdims=True) + norm_eps)

    for q in (1, n_z - 1, 2):
        zq = lax.rem(z + q, n_z)
        arrived(wt.at[d, zq, k, :, la], s_a.at[0, q])
        for i in range(1, n_dp):
            rdma(
                wt.at[d, zq, k, :, la], wt.at[d, zq, k, :, la], s_a.at[n_dp - i, q], dd_of(i), c
            )
    rdma(wt.at[d, :, k, :, la], wt.at[d, :, k, :, la], s_ap.at[0], d, mate)
    for i in range(1, n_z):
        rdma(wt.at[d, z, k, :, lb], wt.at[d, z, k, :, lb], s_bz.at[n_z - i], d, zc(i))
    for r in range(1, n_dp):
        dr = dd_of(r)
        for q in range(n_z):
            arrived(wt.at[dr, lax.rem(z + q, n_z), k, :, la], s_a.at[r, q])
        rdma(wt.at[dr, :, k, :, la], wt.at[dr, :, k, :, la], s_ap.at[r], d, mate)

    gain_all = jnp.zeros((8, model), F32)
    for i in range(1, n_ctx):
        arrived(gb.at[lax.rem(c + i, n_ctx)], s_gain.at[i])
    for e in range(n_ctx):
        piece = widen(gb[e], model)
        gain_all = gain_all + (piece if e == 0 else shift_lanes(piece, shard_rows * e))
    gain1 = gain_all[0:1]
    gain2 = gain_all[1:2]
    normed = (stream * inv1 * gain1).astype(BF)
    na_ref[...] = normed

    kt = kvsum
    for r in range(n_dp):
        arrived(wt.at[dd_of(r), :, 1 - k, :, la], s_ap.at[r])

    def project(e, _):
        w = wt[e, :, :, :, 0:512].reshape(model, 512)
        o = dot_nn(na_ref[...], w)
        o_t = jnp.transpose(o)
        at[pl.ds(pl.multiple_of(e * cq, 32), cq), :] = o_t[:cq]
        kt[pl.ds(pl.multiple_of(e * ck, 32), ck), :] = o_t[cq : cq + ck]
        kt[pl.ds(pl.multiple_of(model // 3 + e * ck, 32), ck), :] = o_t[cq + ck : cq + 2 * ck]
        return 0

    lax.fori_loop(0, n_dp, project, 0)
    cosine = cos_ref[...]
    sine = sin_ref[...]
    half = hs // 2

    def turn(first, second):
        return first * cosine - second * sine, second * cosine + first * sine

    def turn_back(first, second):
        return first * cosine + second * sine, second * cosine - first * sine

    kvw = model // 3
    for g in range(kvh):
        lo, hi = turn(kt[g * hs : g * hs + half], kt[g * hs + half : (g + 1) * hs])
        kvb[c, 128 * g : 128 * g + 64, :] = jnp.concatenate([lo, hi], axis=0).astype(BF)
        kvb[c, 128 * g + 64 : 128 * g + 128, :] = kt[kvw + g * hs : kvw + (g + 1) * hs].astype(BF)
    for i in range(1, n_z):
        rdma(kvb.at[c], kvb.at[c], s_kv.at[n_z - i], d, zc(i))
    rdma(kvb.at[c], kvb.at[c], s_kv.at[n_z], d, mate)
    for h in range(kvh * group):
        lo, hi = turn(at[h * hs : h * hs + half], at[h * hs + half : (h + 1) * hs])
        low = jnp.concatenate([lo, hi], axis=0).astype(BF)
        qt[h * hs : (h + 1) * hs, :] = (low.astype(F32) * 0.125).astype(BF)

    for q in range(1, n_z):
        zq = lax.rem(z + q, n_z)
        arrived(wt.at[d, zq, k, :, lb], s_bz.at[q])
    for i in range(1, n_dp):
        rdma(wt.at[d, :, k, :, lb], wt.at[d, :, k, :, lb], s_b.at[n_dp - i], dd_of(i), c)
    rdma(wt.at[d, :, k, :, lb], wt.at[d, :, k, :, lb], s_bp.at[0], d, mate)
    big_sends = []
    for i in range(1, n_z):
        big_sends.append(
            rdma(big.at[k, 0:2, z], big.at[k, 0:2, z], s_gu.at[n_z - i], d, zc(i))
        )
    for i in range(1, n_z):
        rdma(w_down, wd.at[d, pl.ds(my_down, rf)], s_wd.at[d], z, zc(i))

    @pl.when(d == z)
    def _():
        wd[d, pl.ds(my_down, rf), :] = w_down[...]

    self_down = pltpu.make_async_remote_copy(
        src_ref=w_down,
        dst_ref=wd.at[d, pl.ds(my_down, rf)],
        send_sem=s_send.at[counter[0]],
        recv_sem=s_wd.at[d],
        device_id=(z, c),
        device_id_type=MESH,
    )
    counter[0] += 1

    @pl.when(d != z)
    def _():
        self_down.start()

    for i in range(1, n_dp):
        rdma(cb.at[own], cb.at[n_dp - i - 1], s_c.at[n_dp - i - 1], dd_of(i), c)
    for q in range(1, n_z):
        arrived(kvb.at[zc(q)], s_kv.at[q])
        rdma(kvb.at[zc(q)], kvb.at[zc(q)], s_kv.at[n_z + q], d, mate)
    for r in range(1, n_dp):
        dr = dd_of(r)
        arrived(wt.at[dr, :, k, :, lb], s_b.at[r])
        rdma(wt.at[dr, :, k, :, lb], wt.at[dr, :, k, :, lb], s_bp.at[r], d, mate)
    for q in range(n_z):
        arrived(kvb.at[2 * lax.rem(z + q, n_z) + 1 - k], s_kv.at[n_z + q])

    tpos = c * rows_tok + lax.broadcasted_iota(jnp.int32, (1, rows_tok), 1)
    lim = tpos
    for p in range(PICS):
        s_p = starts[0, p]
        lim = jnp.where((tpos >= s_p) & (tpos < s_p + PIC), jnp.maximum(lim, s_p + PIC - 1), lim)
    lim3 = jnp.concatenate([lim] * group, axis=1)

    def heads_of(ref, g):
        return jnp.concatenate(
            [
                ref[pl.ds(pl.multiple_of(g * group * hs + hs * j, hs), hs), :]
                for j in range(group)
            ],
            axis=1,
        )

    def attend(g, _):
        q_t = heads_of(qt, g)
        q_z = jnp.concatenate([q_t, jnp.zeros_like(q_t)], axis=0)
        k0 = pl.multiple_of(g * 128, 128)
        most = jnp.full((1, gl), -1e30, F32)
        for b in range(n_ctx):
            kv = jnp.transpose(kvb[b, pl.ds(k0, 128), :])
            s = dot_nn(kv, q_z)
            kpos = b * rows_tok + lax.broadcasted_iota(jnp.int32, (rows_tok, gl), 0)
            s = jnp.where(kpos <= lim3, s, -1e30)
            sc[b * rows_tok : (b + 1) * rows_tok, :] = s
            most = jnp.maximum(most, jnp.max(s, axis=0, keepdims=True))
        total = jnp.zeros((1, gl), F32)
        o_t = jnp.zeros((hs, gl), F32)
        for b in range(n_ctx):
            p = jnp.exp(sc[b * rows_tok : (b + 1) * rows_tok, :] - most)
            p_low = p.astype(BF)
            pp[g, b * rows_tok : (b + 1) * rows_tok, :] = p_low
            total = total + jnp.sum(p, axis=0, keepdims=True)
            o_t = o_t + dot_nn(kvb[b, pl.ds(pl.multiple_of(k0 + hs, hs), hs), :], p_low)
        inv = 1.0 / total
        rl[g] = jnp.broadcast_to(inv, (8, gl))
        o_t = o_t * inv
        for j in range(group):
            at[pl.ds(pl.multiple_of(g * group * hs + hs * j, hs), hs), :] = o_t[
                :, rows_tok * j : rows_tok * (j + 1)
            ]
        return 0

    lax.fori_loop(0, kvh, attend, 0)

    big_sends.append(rdma(big.at[k, 0:2, z], big.at[k, 0:2, z], s_gu.at[n_z], d, mate))
    for q in range(1, n_z):
        zq = lax.rem(z + q, n_z)
        arrived(big.at[k, 0:2, zq], s_gu.at[q])
        big_sends.append(
            rdma(big.at[k, 0:2, zq], big.at[k, 0:2, zq], s_gu.at[n_z + q], d, mate)
        )
    for e in range(n_dp):

        @pl.when((d != z) | (d != e))
        def _():
            arrived(wd.at[e, pl.ds(my_down, rf)], s_wd.at[e])

    rdma(wd.at[:, pl.ds(my_down, rf)], wd.at[:, pl.ds(my_down, rf)], s_wd.at[n_dp], d, mate)

    att_t = at[...].astype(BF)
    nat[:, 0:rows_tok] = jnp.transpose(na_ref[...])
    nat[:, rows_tok : 2 * rows_tok] = att_t
    na_ref[...] = jnp.transpose(att_t)
    resid_ref[...] = tok[...].astype(F32)
    for r in range(n_dp):
        arrived(wt.at[dd_of(r), :, 1 - k, :, lb], s_bp.at[r])
    lead = 2 * ck + cq - 384

    def out_block(e, _):
        w = wt[e, :, :, :, 384:pack].reshape(model, pack - 384)
        o = dot_nn(na_ref[...], w)
        lane = lax.broadcasted_iota(jnp.int32, o.shape, 1)
        o = widen(jnp.where(lane >= lead, o, 0.0), model)
        resid_ref[...] += shift_lanes(o, lax.rem(e * cq + model - lead, model))
        return 0

    lax.fori_loop(0, n_dp, out_block, 0)
    resid = resid_ref[...]
    inv2 = lax.rsqrt(jnp.mean(resid * resid, axis=1, keepdims=True) + norm_eps)
    xb[own] = (resid * inv2 * gain2).astype(BF)
    for i in range(1, n_dp):
        rdma(xb.at[own], xb.at[n_dp - i - 1], s_x.at[n_dp - i - 1], dd_of(i), c)
    xt[:, own * rows_tok :] = jnp.transpose(xb[own])
    for q in range(n_z):
        arrived(big.at[1 - k, 0:2, lax.rem(z + q, n_z)], s_gu.at[n_z + q])
    arrived(wd.at[:, pl.ds(its_down, rf)], s_wd.at[n_dp])
    for p in range(n_dp - 1):
        arrived(cb.at[p], s_c.at[p])
    for p in range(n_dp - 1):
        arrived(xb.at[p], s_x.at[p])

    nc = 256

    def weight_cols(e, n0):
        return jnp.concatenate(
            [big[b % 2, e, b // 2, :, pl.ds(n0, nc)] for b in range(n_ctx)], axis=0
        )

    for hf in range(n_dp // 2):
        t0 = 2 * hf
        r0 = t0 * rows_tok
        rh = 2 * rows_tok
        dna[...] = jnp.zeros_like(dna)

        def cols(n, _):
            n0 = pl.multiple_of(n * nc, nc)
            n1 = pl.multiple_of(n * nc + ffs, nc)
            x = xb[t0 : t0 + 2].reshape(rh, model)
            w_g = weight_cols(0, n0)
            w_u = weight_cols(1, n0)
            g = dot_nn(x, w_g)
            u = dot_nn(x, w_u)
            dh = jnp.zeros((rh, nc), F32)
            for e in range(n_dp):
                dh = dh + dot_nt(cb[t0 : t0 + 2, e].reshape(rh, 384), wd[e, pl.ds(n0, nc), :])
            sg = jax.nn.sigmoid(g)
            si = g * sg
            hb[r0 : r0 + rh, pl.ds(n0, nc)] = (si * u).astype(BF)
            dg = (dh * u * sg * (1.0 + g * (1.0 - sg))).astype(BF)
            du = (dh * si).astype(BF)
            dgu[r0 : r0 + rh, pl.ds(n0, nc)] = dg
            dgu[r0 : r0 + rh, pl.ds(n1, nc)] = du
            dna[...] += dot_nt(dg, w_g) + dot_nt(du, w_u)
            return 0

        lax.fori_loop(0, ffs // nc, cols, 0)
        dn[t0 : t0 + 2] = dna[...].astype(BF).reshape(2, rows_tok, model)
        for p in (t0, t0 + 1):
            if p != own:
                there = n_dp - p - 2
                rdma(dn.at[p], drecv.at[there], s_d.at[there], dd_of(p + 1), c)
        for e in range(n_dp):
            y = dot_nn(hb[r0 : r0 + rh, :], wd[e])
            op[t0 : t0 + 2, e] = y.astype(BF).reshape(2, rows_tok, 384)
        for p in (t0, t0 + 1):
            if p != own:
                there = n_dp - p - 2
                rdma(op.at[p], orecv.at[there], s_o.at[there], dd_of(p + 1), c)

    for p in range(n_dp - 1):
        xt[:, p * rows_tok : (p + 1) * rows_tok] = jnp.transpose(xb[p])
    for p in range(n_dp):
        ht[:, p * rows_tok : (p + 1) * rows_tok] = jnp.transpose(
            hb[p * rows_tok : (p + 1) * rows_tok, :]
        )
    for e in range(2):

        def gu_cols(n, _):
            n0 = pl.multiple_of(n * nc, nc)
            n1 = pl.multiple_of(n * nc + e * ffs, nc)
            r = dot_nn(xt[...], dgu[:, pl.ds(n1, nc)]).astype(BF)
            for b in range(n_ctx):
                big[b % 2, 2 + e, b // 2, :, pl.ds(n0, nc)] = r[
                    shard_rows * b : shard_rows * (b + 1)
                ]
            return 0

        lax.fori_loop(0, ffs // nc, gu_cols, 0)
    big_sends.append(rdma(big.at[1 - k, 2:4], gu_r, s_gur.at[0], d, mate))

    def gd_cols(e, _):
        r = dot_nn(ht[...], cb[:, e].reshape(n_dp * rows_tok, 384)).astype(BF)
        for j in range(2):
            gd[j, e] = r[rf * j : rf * (j + 1)]
        return 0

    lax.fori_loop(0, n_dp, gd_cols, 0)
    rdma(gd.at[1 - k], gd_r, s_gdr.at[0], d, mate)

    for p in range(n_dp - 1):
        arrived(drecv.at[p], s_d.at[p])
    d_nm = dna[rows_tok : 2 * rows_tok, :]
    for p in range(n_dp - 1):
        d_nm = d_nm + drecv[p].astype(F32)

    def norm_out(inputs, inverse, gain_vec, upstream):
        scaled = gain_vec * upstream
        return inverse * scaled - inputs * inverse * inverse * inverse * jnp.mean(
            scaled * inputs, axis=1, keepdims=True
        )

    resid = resid_ref[...]
    ggs[1:2, :] = jnp.sum(d_nm * resid * inv2, axis=0, keepdims=True)
    d_res = cot[...].astype(F32) + norm_out(resid, inv2, gain2, d_nm)
    gres[...] = d_res
    d_low = d_res.astype(BF).astype(F32)
    o0 = 2 * ck + cq
    for e in range(n_dp):
        t = shift_lanes(d_low, (o0 - cq * e) % model)[:, :pack]
        lane = lax.broadcasted_iota(jnp.int32, t.shape, 1)
        rb[e, rows_tok : 2 * rows_tok, :] = jnp.where(lane >= o0, t, 0.0).astype(BF)
    dna[...] = jnp.zeros_like(dna)

    def att_block(e, _):
        w = wt[e, :, :, :, 384:pack].reshape(model, pack - 384)
        dna[0:rows_tok, :] += dot_nt(rb[e, rows_tok : 2 * rows_tok, 384:pack], w)
        return 0

    lax.fori_loop(0, n_dp, att_block, 0)
    dat[...] = jnp.transpose(dna[0:rows_tok, :].astype(BF))

    arrived(gu_r, s_gur.at[0])

    def gu_sum(n, _):
        e = n // n_z
        j = lax.rem(n, n_z)
        gu_r[e, j] = (gu_r[e, j].astype(F32) + big[k, 2 + e, j].astype(F32)).astype(BF)
        return 0

    lax.fori_loop(0, 2 * n_z, gu_sum, 0)
    for i in range(1, n_z):
        there = n_z - i - 1
        rdma(
            gu_r.at[:, lax.rem(z + i, n_z)], gu_z.at[there], s_gur.at[there + 1], d, zc(i)
        )
    arrived(gd_r, s_gdr.at[0])

    def gd_sum(e, _):
        gd_r[e] = (gd_r[e].astype(F32) + gd[k, e].astype(F32)).astype(BF)
        return 0

    lax.fori_loop(0, n_dp, gd_sum, 0)
    for i in range(1, n_dp):
        rdma(gd_r.at[dd_of(i)], gd_z.at[z], s_gdz.at[z], dd_of(i), 2 * d + k)

    @pl.when(d == z)
    def _():
        gd_z[z] = gd_r[d]

    self_grad = pltpu.make_async_remote_copy(
        src_ref=gd_r.at[d],
        dst_ref=gd_z.at[z],
        send_sem=s_send.at[counter[0]],
        recv_sem=s_gdz.at[z],
        device_id=(d, 2 * d + k),
        device_id_type=MESH,
    )
    counter[0] += 1

    @pl.when(d != z)
    def _():
        self_grad.start()

    def attend_back(g, _):
        q_t = heads_of(qt, g)
        a_t = heads_of(dat, g)
        o_t = heads_of(at, g)
        none = jnp.zeros_like(q_t)
        inv = rl[g][0:1]
        delta = jnp.sum(a_t.astype(F32) * o_t, axis=0, keepdims=True) * inv
        a_z = jnp.concatenate([none, a_t], axis=0)
        a_inv = (a_t.astype(F32) * inv).astype(BF)
        q2 = jnp.transpose(jnp.concatenate([q_t, none], axis=0))
        a2 = jnp.transpose(jnp.concatenate([none, a_inv], axis=0))
        k0 = pl.multiple_of(g * 128, 128)
        dq = jnp.zeros((hs, gl), F32)
        for b in range(n_ctx):
            kv_t = kvb[b, pl.ds(k0, 128), :]
            dp = dot_nn(jnp.transpose(kv_t), a_z)
            p_low = pp[g, b * rows_tok : (b + 1) * rows_tok, :]
            ds = (p_low.astype(F32) * (dp * inv - delta)).astype(BF)
            dq = dq + dot_nn(kv_t[:hs], ds)
            both = dot_nn(ds, q2) + dot_nn(p_low, a2)
            dkv[b % 2, b // 2, pl.ds(k0, 128), :] = jnp.transpose(both).astype(BF)
        dq = dq * 0.125
        for j in range(group):
            at[pl.ds(pl.multiple_of(g * group * hs + hs * j, hs), hs), :] = dq[
                :, rows_tok * j : rows_tok * (j + 1)
            ]
        return 0

    lax.fori_loop(0, kvh, attend_back, 0)
    rdma(dkv.at[1 - k], dkv_r, s_dkv.at[0], d, mate)
    for h in range(kvh * group):
        lo, hi = turn_back(at[h * hs : h * hs + half], at[h * hs + half : (h + 1) * hs])
        qt[h * hs : (h + 1) * hs, :] = jnp.concatenate([lo, hi], axis=0).astype(BF)
    arrived(dkv_r, s_dkv.at[0])

    def kv_sum(j, _):
        dkv_r[j] = (dkv_r[j].astype(F32) + dkv[k, j].astype(F32)).astype(BF)
        return 0

    lax.fori_loop(0, n_z, kv_sum, 0)
    for i in range(1, n_z):
        there = n_z - i - 1
        rdma(dkv_r.at[lax.rem(z + i, n_z)], dkv_z.at[there], s_dkv.at[there + 1], d, zc(i))

    for p in range(n_dp - 1):
        arrived(orecv.at[p], s_o.at[p])
    y_all = resid_ref[...]
    for e in range(n_dp):
        y = op[own, e].astype(F32)
        for p in range(n_dp - 1):
            y = y + orecv[p, e].astype(F32)
        y = widen(y, model)
        y_all = y_all + (y if e == 0 else shift_lanes(y, cq * e))
    out_ref[...] = y_all.astype(BF)
    for copy in big_sends:
        copy.wait_send()
    pending[:] = [copy for copy in pending if all(copy is not other for other in big_sends)]

    for i in range(n_z - 1):
        arrived(dkv_z.at[i], s_dkv.at[i + 1])
    kv_total = dkv_r[z].astype(F32)
    for i in range(n_z - 1):
        kv_total = kv_total + dkv_z[i].astype(F32)
    kvsum[...] = kv_total
    for g in range(kvh):
        r = 128 * g
        lo, hi = turn_back(kvsum[r : r + half], kvsum[r + half : r + hs])
        at[g * hs : (g + 1) * hs, :] = jnp.concatenate([lo, hi], axis=0)
        at[kvw + g * hs : kvw + (g + 1) * hs, :] = kvsum[r + hs : r + 2 * hs]
    for e in range(n_dp):
        rows = jnp.concatenate(
            [
                qt[cq * e : cq * (e + 1)],
                at[ck * e : ck * (e + 1)].astype(BF),
                at[kvw + ck * e : kvw + ck * (e + 1)].astype(BF),
                jnp.zeros((512 - o0, rows_tok), BF),
            ],
            axis=0,
        )
        rb[e, 0:rows_tok, :] = widen(jnp.transpose(rows), pack)

    for r in (1, 2, 3, 0):
        e = dd_of(r)

        def pack_cols(n, _):
            n0 = pl.multiple_of(n * nc, nc)
            t = dot_nn(nat[...], rb[e, :, pl.ds(n0, nc)]).astype(BF)
            for b in range(n_ctx):
                big[b % 2, e, b // 2, :, pl.ds(n0, nc)] = t[
                    shard_rows * b : shard_rows * (b + 1)
                ]
            return 0

        lax.fori_loop(0, pack // nc, pack_cols, 0)
        rdma(big.at[1 - k, e], g_r.at[e], s_gr.at[r], d, mate)

    def chip_sum(r):
        e = dd_of(r)
        arrived(g_r.at[e], s_gr.at[r])

        def one(j, _):
            g_r[e, j] = (g_r[e, j].astype(F32) + big[k, e, j].astype(F32)).astype(BF)
            return 0

        lax.fori_loop(0, n_z, one, 0)
        return e

    for r in range(1, n_dp):
        e = chip_sum(r)
        there = n_dp - r - 1
        rdma(g_r.at[e], g_p.at[there], s_gp.at[there], e, c)

    dna[...] = jnp.zeros_like(dna)

    def in_block(e, _):
        w = wt[e, :, :, :, 0:512].reshape(model, 512)
        dna[0:rows_tok, :] += dot_nt(rb[e, 0:rows_tok, 0:512], w)
        return 0

    lax.fori_loop(0, n_dp, in_block, 0)
    d_na = dna[0:rows_tok, :]
    stream = tok[...].astype(F32)
    ggs[0:1, :] = jnp.sum(d_na * stream * inv1, axis=0, keepdims=True)
    ig_ref[...] = gres[...] + norm_out(stream, inv1, gain1, d_na)
    for i in range(1, n_dp):
        there = n_dp - i - 1
        rdma(ggs, gg_p.at[there], s_ggp.at[there], dd_of(i), c)
    chip_sum(0)
    for p in range(n_dp - 1):
        arrived(gg_p.at[p], s_ggp.at[p])
    gg_all = ggs[...]
    for p in range(n_dp - 1):
        gg_all = gg_all + gg_p[p]
    gg_c[0] = gg_all
    for i in range(1, n_ctx):
        rdma(gg_c.at[0], gg_c.at[n_ctx - i], s_ggc.at[n_ctx - i], d, lax.rem(c + i, n_ctx))
    for i in range(n_z - 1):
        arrived(gu_z.at[i], s_gur.at[i + 1])
    for e in range(2):
        t = gu_r[e, z].astype(F32)
        for i in range(n_z - 1):
            t = t + gu_z[i, e].astype(F32)
        g_gu_ref[e] = t
    for j in range(n_z):

        @pl.when((d != z) | (z != j))
        def _():
            arrived(gd_z.at[j], s_gdz.at[j])

    t = gd_z[0].astype(F32)
    for j in range(1, n_z):
        t = t + gd_z[j].astype(F32)
    g_down_ref[...] = t
    for p in range(n_dp - 1):
        arrived(g_p.at[p], s_gp.at[p])

    def plane_sum(j):
        t = g_r[d, j].astype(F32)
        for p in range(n_dp - 1):
            t = t + g_p[p, j].astype(F32)
        return t

    for i in range(1, n_z):
        zq = lax.rem(z + i, n_z)
        there = n_z - i - 1
        g_r[d, zq] = plane_sum(zq).astype(BF)
        rdma(g_r.at[d, zq], g_z.at[there], s_gz.at[there], d, zc(i))
    g_pack_ref[...] = plane_sum(z)
    for i in range(1, n_ctx):
        arrived(gg_c.at[i], s_ggc.at[i])
    gg_tot = gg_c[0]
    for i in range(1, n_ctx):
        gg_tot = gg_tot + gg_c[i]
    gg_ref[...] = shift_lanes(gg_tot, lax.rem(model - shard_rows * c, model))[:, :256]
    for i in range(n_z - 1):
        arrived(g_z.at[i], s_gz.at[i])
    t = g_pack_ref[...]
    for i in range(n_z - 1):
        t = t + g_z[i].astype(F32)
    g_pack_ref[...] = t
    for copy in pending:
        copy.wait_send()

    @pl.when(d != z)
    def _():
        self_down.wait_send()
        self_grad.wait_send()
def fast_body(
    n_dp,
    n_ctx,
    tokens,
    starts,
    gain_attn,
    gain_mlp,
    w_query,
    w_key,
    w_value,
    w_out,
    w_gate,
    w_up,
    w_down,
    cotangent,
):
    n_z = n_ctx // 2
    rows_tok, model = tokens.shape[1:]
    sr = w_query.shape[0]
    rf, cd = w_down.shape
    ffs = w_gate.shape[1]
    cq = w_query.shape[1]
    ck = w_key.shape[1]
    pack = 2 * (cq + ck)
    length = rows_tok * n_ctx
    gl = 3 * rows_tok
    packed = jnp.concatenate([w_query, w_key, w_value, w_out], axis=1)
    down = jnp.pad(w_down, ((0, 0), (0, 384 - cd)))
    gains = jnp.pad(
        jnp.stack([gain_attn, gain_mlp]).astype(jnp.float32), ((0, 6), (0, 256 - sr))
    )
    half = HEAD_SIZE // 2
    positions = lax.axis_index("ctx") * rows_tok + jnp.arange(rows_tok)
    freqs = 10000.0 ** (-jnp.arange(half).astype(jnp.float32) / half)
    angles = freqs[:, None] * positions.astype(jnp.float32)[None, :]
    vm = pl.BlockSpec(memory_space=pltpu.VMEM)
    dma = pltpu.SemaphoreType.DMA
    n = n_dp - 1
    m = n_z - 1
    scratch = [
        pltpu.VMEM((n_ctx, 8, 256), F32),
        pltpu.VMEM((n_dp, n_z, 2, sr, pack), BF),
        pltpu.VMEM((2, n_dp, n_z, sr, ffs), BF),
        pltpu.VMEM((n_dp, 2 * rf, 384), BF),
        pltpu.VMEM((rows_tok, model), BF),
        pltpu.VMEM((model, rows_tok), BF),
        pltpu.VMEM((n_ctx, 2 * model // 3, rows_tok), BF),
        pltpu.VMEM((length, gl), F32),
        pltpu.VMEM((6, length, gl), BF),
        pltpu.VMEM((6, 8, gl), F32),
        pltpu.VMEM((model, rows_tok), F32),
        pltpu.VMEM((rows_tok, model), F32),
        pltpu.VMEM((n_dp, rows_tok, model), BF),
        pltpu.VMEM((n_dp, n_dp, rows_tok, 384), BF),
        pltpu.VMEM((n_dp, n_dp, rows_tok, 384), BF),
        pltpu.VMEM((n, n_dp, rows_tok, 384), BF),
        pltpu.VMEM((n_dp, rows_tok, model), BF),
        pltpu.VMEM((n, rows_tok, model), BF),
        pltpu.VMEM((2 * rows_tok, model), F32),
        pltpu.VMEM((n_dp * rows_tok, ffs), BF),
        pltpu.VMEM((n_dp * rows_tok, 2 * ffs), BF),
        pltpu.VMEM((model, n_dp * rows_tok), BF),
        pltpu.VMEM((ffs, n_dp * rows_tok), BF),
        pltpu.VMEM((rows_tok, model), F32),
        pltpu.VMEM((model, rows_tok), BF),
        pltpu.VMEM((n_dp, 2 * rows_tok, pack), BF),
        pltpu.VMEM((2, n_z, 2 * model // 3, rows_tok), BF),
        pltpu.VMEM((n_z, 2 * model // 3, rows_tok), BF),
        pltpu.VMEM((m, 2 * model // 3, rows_tok), BF),
        pltpu.VMEM((2 * model // 3, rows_tok), F32),
        pltpu.VMEM((2, n_z, sr, ffs), BF),
        pltpu.VMEM((m, 2, sr, ffs), BF),
        pltpu.VMEM((2, n_dp, rf, 384), BF),
        pltpu.VMEM((n_dp, rf, 384), BF),
        pltpu.VMEM((n_z, rf, 384), BF),
        pltpu.VMEM((n_dp, n_z, sr, pack), BF),
        pltpu.VMEM((n, n_z, sr, pack), BF),
        pltpu.VMEM((m, sr, pack), BF),
        pltpu.VMEM((model, 2 * rows_tok), BF),
        pltpu.VMEM((8, model), F32),
        pltpu.VMEM((n, 8, model), F32),
        pltpu.VMEM((n_ctx, 8, model), F32),
        dma((130,)),
        dma((n_ctx,)),
        dma((n_dp, n_z)),
        dma((n_dp,)),
        dma((n_dp,)),
        dma((n_z,)),
        dma((n_dp,)),
        dma((2 * n_z,)),
        dma((2 * n_z,)),
        dma((n_dp + 1,)),
        dma((n,)),
        dma((n,)),
        dma((n,)),
        dma((n,)),
        dma((n_z,)),
        dma((n_z,)),
        dma((1,)),
        dma((n_z,)),
        dma((n_dp,)),
        dma((n,)),
        dma((m,)),
        dma((n,)),
        dma((n_ctx,)),
    ]
    out, ig, gg, g_pack, g_gu, g_down = pl.pallas_call(
        functools.partial(fast_kernel, n_dp, n_ctx),
        out_shape=(
            jax.ShapeDtypeStruct((rows_tok, model), BF),
            jax.ShapeDtypeStruct((rows_tok, model), F32),
            jax.ShapeDtypeStruct((8, 256), F32),
            jax.ShapeDtypeStruct((sr, pack), F32),
            jax.ShapeDtypeStruct((2, sr, ffs), F32),
            jax.ShapeDtypeStruct((rf, 384), F32),
        ),
        in_specs=[vm, vm, pl.BlockSpec(memory_space=pltpu.SMEM)] + [vm] * 7,
        out_specs=(vm,) * 6,
        scratch_shapes=scratch,
        compiler_params=pltpu.CompilerParams(
            has_side_effects=True, vmem_limit_bytes=67043328
        ),
        name="layer",
    )(
        tokens[0],
        cotangent[0],
        starts,
        gains,
        jnp.cos(angles),
        jnp.sin(angles),
        packed,
        w_gate,
        w_up,
        down,
    )
    return (
        out[None],
        ig[None],
        gg[0, :sr],
        gg[1, :sr],
        g_pack[:, :cq],
        g_pack[:, cq : cq + ck],
        g_pack[:, cq + ck : cq + 2 * ck],
        g_pack[:, cq + 2 * ck :],
        g_gu[0],
        g_gu[1],
        g_down[:, :cd],
    )


def solution(mesh):
    n_dp = mesh.shape["dp"]
    n_ctx = mesh.shape["ctx"]

    def choose(tokens, *rest):
        fits = n_dp == 4 and n_ctx == 2 * n_dp and tokens.shape[1:] == (128, 1152)
        if fits:
            return fast_body(n_dp, n_ctx, tokens, *rest)
        return body(tokens, *rest)

    return jax.shard_map(
        choose,
        mesh=mesh,
        in_specs=(
            P("dp", "ctx", None),
            P("dp", None),
            P("ctx"),
            P("ctx"),
            P("ctx", "dp"),
            P("ctx", "dp"),
            P("ctx", "dp"),
            P("ctx", "dp"),
            P("ctx", "dp"),
            P("ctx", "dp"),
            P("ctx", "dp"),
            P("dp", "ctx", None),
        ),
        out_specs=(
            P("dp", "ctx", None),
            P("dp", "ctx", None),
            P("ctx"),
            P("ctx"),
            P("ctx", "dp"),
            P("ctx", "dp"),
            P("ctx", "dp"),
            P("ctx", "dp"),
            P("ctx", "dp"),
            P("ctx", "dp"),
            P("ctx", "dp"),
        ),
        check_vma=False,
    )
```

```python
import functools

import jax
import jax.numpy as jnp
from jax import lax
from jax.experimental import pallas as pl
from jax.experimental.pallas import tpu as pltpu
from jax.sharding import PartitionSpec as P

HEAD_SIZE = 64
PIC = 256
PICS = 4


norm_eps = 1e-05


def rotary_embedding(field, token_positions):
    half = field.shape[-1] // 2
    freqs = 10000.0 ** (-jnp.arange(half).astype(jnp.float32) / half)
    angles = token_positions.astype(jnp.float32)[:, None] * freqs[None, :]
    cosine = jnp.cos(angles)[:, None, :]
    sine = jnp.sin(angles)[:, None, :]
    first = field[..., :half]
    second = field[..., half:]
    return jnp.concatenate(
        [first * cosine - second * sine, second * cosine + first * sine], axis=-1
    )


def rotary_back(field, token_positions):
    half = field.shape[-1] // 2
    freqs = 10000.0 ** (-jnp.arange(half).astype(jnp.float32) / half)
    angles = token_positions.astype(jnp.float32)[:, None] * freqs[None, :]
    cosine = jnp.cos(angles)[:, None, :]
    sine = jnp.sin(angles)[:, None, :]
    first = field[..., :half]
    second = field[..., half:]
    return jnp.concatenate(
        [first * cosine + second * sine, second * cosine - first * sine], axis=-1
    )


def piece_ids(token_positions, seq_starts):
    inside = (token_positions[:, None] >= seq_starts[None, :]) & (
        token_positions[:, None] < seq_starts[None, :] + PIC
    )
    labels = jnp.arange(1, PICS + 1)
    return jnp.sum(jnp.where(inside, labels[None, :], 0), axis=1) - 1


def norm_back(inputs, inverse, gain_vec, upstream):
    scaled = gain_vec * upstream
    return inverse * scaled - inputs * inverse**3 * jnp.mean(
        scaled * inputs, axis=-1, keepdims=True
    )


def fetch_weights(gain_attn, gain_mlp, w_query, w_key, w_value, w_out, w_gate, w_up, w_down):
    packed = jnp.concatenate([w_query, w_key, w_value, w_out], axis=1)
    gains = lax.all_gather(jnp.stack([gain_attn, gain_mlp]), "ctx", axis=1, tiled=True)
    packed = lax.all_gather(packed, ("dp", "ctx"), axis=0, tiled=True)
    packed = packed.reshape(lax.axis_size("dp"), -1, packed.shape[1])
    gate_up = lax.all_gather(jnp.concatenate([w_gate, w_up], axis=1), "ctx", axis=0, tiled=True)
    down = lax.all_gather(w_down, "ctx", axis=0, tiled=True)
    cuts = []
    first = 0
    for shard in (w_query, w_key, w_value, w_out):
        part = packed[:, :, first : first + shard.shape[1]]
        cuts.append(jnp.transpose(part, (1, 0, 2)).reshape(part.shape[1], -1))
        first += shard.shape[1]
    ff = w_gate.shape[1]
    return (gains[0], gains[1], *cuts, gate_up[:, :ff], gate_up[:, ff:], down)


def gather_keys(key_rot, value_low):
    return (
        lax.all_gather(key_rot, "ctx", axis=0, tiled=True),
        lax.all_gather(value_low, "ctx", axis=0, tiled=True),
    )


def delta_of(grad_rows, attended_rows):
    return jnp.transpose(jnp.sum(grad_rows.astype(jnp.float32) * attended_rows, axis=-1), (1, 2, 0))


def as_rows(stat):
    return jnp.transpose(stat, (2, 0, 1)).reshape(stat.shape[2], -1)


def body(
    tokens,
    starts,
    gain_attn,
    gain_mlp,
    w_query,
    w_key,
    w_value,
    w_out,
    w_gate,
    w_up,
    w_down,
    cotangent,
):
    tok_count = tokens.shape[1]
    length = tok_count * lax.axis_size("ctx")
    span = min(512, length)
    n_blocks = length // span
    query_pos = lax.axis_index("ctx") * tok_count + jnp.arange(tok_count)
    seq_starts = starts[0]
    labels_all = piece_ids(jnp.arange(length), seq_starts)

    def reach_of(token_positions):
        inside = (token_positions[:, None] >= seq_starts[None, :]) & (
            token_positions[:, None] < seq_starts[None, :] + PIC
        )
        return jnp.maximum(
            token_positions[-1], jnp.max(jnp.where(inside, seq_starts[None, :] + PIC - 1, -1))
        )

    gathered = fetch_weights(
        gain_attn, gain_mlp, w_query, w_key, w_value, w_out, w_gate, w_up, w_down
    )
    (
        gain_first,
        gain_second,
        mat_query,
        key_projection,
        value_projection,
        mat_out,
        mat_gate,
        mat_up,
        mat_down,
    ) = gathered
    heads_kv = key_projection.shape[1] // HEAD_SIZE
    group_size = mat_query.shape[1] // key_projection.shape[1]
    score_scale = HEAD_SIZE ** (-0.5)
    gain_one = gain_first.astype(jnp.float32)
    gain_two = gain_second.astype(jnp.float32)
    stream = tokens[0].astype(jnp.float32)
    inv_one = lax.rsqrt(jnp.mean(stream * stream, axis=-1, keepdims=True) + norm_eps)
    attention_normed = (stream * inv_one * gain_one).astype(jnp.bfloat16)
    query_unrotated = jnp.dot(attention_normed, mat_query, preferred_element_type=jnp.float32)
    key_unrotated = jnp.dot(attention_normed, key_projection, preferred_element_type=jnp.float32)
    v_pre = jnp.dot(attention_normed, value_projection, preferred_element_type=jnp.float32)
    query_vectors = (
        rotary_embedding(query_unrotated.reshape(tok_count, -1, HEAD_SIZE), query_pos)
        .astype(jnp.bfloat16)
        .reshape(tok_count, -1)
    )
    key_rot = (
        rotary_embedding(key_unrotated.reshape(tok_count, heads_kv, HEAD_SIZE), query_pos)
        .astype(jnp.bfloat16)
        .reshape(tok_count, -1)
    )
    value_low = v_pre.astype(jnp.bfloat16)
    key_all, value_all = gather_keys(key_rot, value_low)

    def key_block(source, block_index):
        return lax.dynamic_slice_in_dim(source, block_index * span, span, 0).reshape(
            span, heads_kv, HEAD_SIZE
        )

    def scores_at(block_index, key_piece, query_set, row_pos, row_lab):
        first_key = block_index * span
        key_pos = first_key + jnp.arange(span)
        key_lab = lax.dynamic_slice_in_dim(labels_all, first_key, span, 0)
        raw = (
            jnp.einsum("qhgd,khd->hgqk", query_set, key_piece, preferred_element_type=jnp.float32)
            * score_scale
        )
        allowed = (key_pos[None, :] <= row_pos[:, None]) | (
            row_lab[:, None] == key_lab[None, :]
        ) & (row_lab[:, None] >= 0)
        return jnp.where(allowed[None, None], raw, -1e30)

    keys_now = key_all
    values_now = value_all
    rows = query_vectors.shape[0]
    query_set = query_vectors.reshape(rows, heads_kv, group_size, HEAD_SIZE)
    row_lab = piece_ids(query_pos, seq_starts)
    reach = reach_of(query_pos)

    def lse_step(running, block_index):

        def lse_live(pair_now):
            most_now, sum_now = pair_now
            masked = scores_at(
                block_index, key_block(keys_now, block_index), query_set, query_pos, row_lab
            )
            most_new = jnp.maximum(most_now, jnp.max(masked, axis=-1))
            sum_new = sum_now * jnp.exp(most_now - most_new) + jnp.sum(
                jnp.exp(masked - most_new[..., None]), axis=-1
            )
            return (most_new, sum_new)

        return (
            lax.cond(block_index * span <= reach, lse_live, lambda pair_now: pair_now, running),
            None,
        )

    start_pair = (
        jnp.full((heads_kv, group_size, rows), -1e30, jnp.float32),
        jnp.zeros((heads_kv, group_size, rows), jnp.float32),
    )
    (most_all, sum_all), _ = lax.scan(lse_step, start_pair, jnp.arange(n_blocks))
    log_norm = most_all + jnp.log(sum_all)

    def out_step(running, block_index):

        def out_live(acc_now):
            masked = scores_at(
                block_index, key_block(keys_now, block_index), query_set, query_pos, row_lab
            )
            chances = jnp.exp(masked - log_norm[..., None]).astype(jnp.bfloat16)
            return acc_now + jnp.einsum(
                "hgqk,khd->qhgd",
                chances,
                key_block(values_now, block_index),
                preferred_element_type=jnp.float32,
            )

        return (
            lax.cond(block_index * span <= reach, out_live, lambda acc_now: acc_now, running),
            None,
        )

    attended_set, _ = lax.scan(
        out_step,
        jnp.zeros((rows, heads_kv, group_size, HEAD_SIZE), jnp.float32),
        jnp.arange(n_blocks),
    )
    att_low = attended_set.reshape(tok_count, -1).astype(jnp.bfloat16)
    resid = stream + jnp.dot(att_low, mat_out, preferred_element_type=jnp.float32)
    inv_two = lax.rsqrt(jnp.mean(resid * resid, axis=-1, keepdims=True) + norm_eps)
    normed_m = (resid * inv_two * gain_two).astype(jnp.bfloat16)
    width = mat_down.shape[1]
    group_normed = lax.all_gather(normed_m, "dp", axis=0, tiled=True)
    grad_low = cotangent[0]
    group_cot = lax.all_gather(grad_low, "dp", axis=0, tiled=True)
    cot_cols = lax.dynamic_slice_in_dim(group_cot, lax.axis_index("dp") * width, width, 1)
    grad_hidden_part = jnp.einsum(
        "td,fd->tf", cot_cols, mat_down, preferred_element_type=jnp.float32
    ).astype(jnp.bfloat16)
    grad_hidden = lax.psum_scatter(
        grad_hidden_part, "dp", scatter_dimension=1, tiled=True
    ).astype(jnp.float32)
    gate_pre = jnp.dot(group_normed, mat_gate, preferred_element_type=jnp.float32)
    up_pre = jnp.dot(group_normed, mat_up, preferred_element_type=jnp.float32)
    sigma = jax.nn.sigmoid(gate_pre)
    silu_val = gate_pre * sigma
    hidden = (silu_val * up_pre).astype(jnp.bfloat16)
    hidden_all = lax.all_gather(hidden, "dp", axis=1, tiled=True)
    down_cols = jnp.dot(hidden_all, mat_down, preferred_element_type=jnp.float32)
    down_rows = lax.all_to_all(
        down_cols.astype(jnp.bfloat16), "dp", split_axis=0, concat_axis=1, tiled=True
    )
    output = (resid + down_rows.astype(jnp.float32)).astype(jnp.bfloat16)
    grad_resid = grad_low.astype(jnp.float32)
    grad_down = jnp.einsum("tf,td->fd", hidden_all, cot_cols, preferred_element_type=jnp.float32)
    grad_gate_pre = (grad_hidden * up_pre * sigma * (1.0 + gate_pre * (1.0 - sigma))).astype(
        jnp.bfloat16
    )
    grad_up_pre = (grad_hidden * silu_val).astype(jnp.bfloat16)
    grad_gate = jnp.einsum(
        "td,tf->df", group_normed, grad_gate_pre, preferred_element_type=jnp.float32
    )
    grad_up = jnp.einsum(
        "td,tf->df", group_normed, grad_up_pre, preferred_element_type=jnp.float32
    )
    grad_nm = jnp.einsum("tf,df->td", grad_gate_pre, mat_gate, preferred_element_type=jnp.float32)
    grad_nm = grad_nm + jnp.einsum(
        "tf,df->td", grad_up_pre, mat_up, preferred_element_type=jnp.float32
    )
    grad_nm = lax.psum_scatter(
        grad_nm.astype(jnp.bfloat16), "dp", scatter_dimension=0, tiled=True
    ).astype(jnp.float32)
    grad_gain_two = jnp.sum(grad_nm * resid * inv_two, axis=0)
    grad_resid = grad_resid + norm_back(resid, inv_two, gain_two, grad_nm)
    grad_branch = grad_resid.astype(jnp.bfloat16)
    grad_wo = jnp.einsum("tq,td->qd", att_low, grad_branch, preferred_element_type=jnp.float32)
    grad_att = jnp.einsum(
        "td,qd->tq", grad_branch, mat_out, preferred_element_type=jnp.float32
    ).astype(jnp.bfloat16)
    delta_all = delta_of(grad_att.reshape(tok_count, heads_kv, group_size, HEAD_SIZE), attended_set)
    back_keys_now = key_all
    back_values_now = value_all
    rows = query_vectors.shape[0]
    back_query_set = query_vectors.reshape(rows, heads_kv, group_size, HEAD_SIZE)
    grad_set = grad_att.reshape(rows, heads_kv, group_size, HEAD_SIZE)
    back_row_lab = piece_ids(query_pos, seq_starts)
    back_reach = reach_of(query_pos)

    def back_step(running, block_index):

        def back_live(dq_acc):
            key_piece = key_block(back_keys_now, block_index)
            value_piece = key_block(back_values_now, block_index)
            masked = scores_at(block_index, key_piece, back_query_set, query_pos, back_row_lab)
            chances = jnp.exp(masked - log_norm[..., None])
            upstream = jnp.einsum(
                "qhgd,khd->hgqk", grad_set, value_piece, preferred_element_type=jnp.float32
            )
            score_grad = (chances * (upstream - delta_all[..., None])).astype(jnp.bfloat16)
            key_grad = score_scale * jnp.einsum(
                "hgqk,qhgd->khd", score_grad, back_query_set, preferred_element_type=jnp.float32
            )
            value_grad = jnp.einsum(
                "hgqk,qhgd->khd",
                chances.astype(jnp.bfloat16),
                grad_set,
                preferred_element_type=jnp.float32,
            )
            dq_new = dq_acc + score_scale * jnp.einsum(
                "hgqk,khd->qhgd", score_grad, key_piece, preferred_element_type=jnp.float32
            )
            return dq_new, (key_grad.astype(jnp.bfloat16), value_grad.astype(jnp.bfloat16))

        none_grad = jnp.zeros((span, heads_kv, HEAD_SIZE), jnp.bfloat16)
        return lax.cond(
            block_index * span <= back_reach,
            back_live,
            lambda dq_acc: (dq_acc, (none_grad, none_grad)),
            running,
        )

    dq_set, kv_parts = lax.scan(
        back_step,
        jnp.zeros((rows, heads_kv, group_size, HEAD_SIZE), jnp.float32),
        jnp.arange(n_blocks),
    )
    dq_low = (
        rotary_back(dq_set.reshape(rows, -1, HEAD_SIZE), query_pos)
        .reshape(rows, -1)
        .astype(jnp.bfloat16)
    )
    kv_parts = jnp.concatenate([part.reshape(length, -1) for part in kv_parts], axis=1)
    kv_sums = lax.psum_scatter(kv_parts, "ctx", scatter_dimension=0, tiled=True).astype(jnp.float32)
    key_grads = kv_sums[:, : heads_kv * HEAD_SIZE].reshape(tok_count, heads_kv, HEAD_SIZE)
    value_grads = kv_sums[:, heads_kv * HEAD_SIZE :]
    dk_low = rotary_back(key_grads, query_pos).reshape(tok_count, -1).astype(jnp.bfloat16)
    dv_low = value_grads.reshape(tok_count, -1).astype(jnp.bfloat16)
    grad_wq = jnp.einsum("td,tq->dq", attention_normed, dq_low, preferred_element_type=jnp.float32)
    grad_wk = jnp.einsum("td,tq->dq", attention_normed, dk_low, preferred_element_type=jnp.float32)
    grad_wv = jnp.einsum("td,tq->dq", attention_normed, dv_low, preferred_element_type=jnp.float32)
    grad_na = jnp.einsum("tq,dq->td", dq_low, mat_query, preferred_element_type=jnp.float32)
    grad_na = grad_na + jnp.einsum(
        "tq,dq->td", dk_low, key_projection, preferred_element_type=jnp.float32
    )
    grad_na = grad_na + jnp.einsum(
        "tq,dq->td", dv_low, value_projection, preferred_element_type=jnp.float32
    )
    grad_gain_one = jnp.sum(grad_na * stream * inv_one, axis=0)
    input_grad = grad_resid + norm_back(stream, inv_one, gain_one, grad_na)
    n_dp = lax.axis_size("dp")
    n_ctx = lax.axis_size("ctx")
    cut = jnp.concatenate(
        [
            jnp.transpose(
                part.astype(jnp.bfloat16).reshape(part.shape[0], n_dp, -1), (1, 0, 2)
            )
            for part in (grad_wq, grad_wk, grad_wv, grad_wo)
        ],
        axis=2,
    )
    mine = lax.psum_scatter(
        cut.reshape(-1, cut.shape[2]), ("dp", "ctx"), scatter_dimension=0, tiled=True
    ).astype(jnp.float32)
    gate_up_sum = lax.psum_scatter(
        jnp.concatenate([grad_gate, grad_up], axis=1).astype(jnp.bfloat16),
        "ctx",
        scatter_dimension=0,
        tiled=True,
    ).astype(jnp.float32)
    down_sum = lax.psum_scatter(
        grad_down.astype(jnp.bfloat16), "ctx", scatter_dimension=0, tiled=True
    ).astype(jnp.float32)
    ff = w_gate.shape[1]
    e_one = w_query.shape[1]
    e_two = e_one + w_key.shape[1]
    e_three = e_two + w_value.shape[1]
    shards = (
        mine[:, :e_one],
        mine[:, e_one:e_two],
        mine[:, e_two:e_three],
        mine[:, e_three:],
        gate_up_sum[:, :ff],
        gate_up_sum[:, ff:],
        down_sum,
    )
    gain_both = lax.psum(jnp.stack([grad_gain_one, grad_gain_two]), ("dp", "ctx"))
    gain_rows = gain_attn.shape[0]
    gain_sums = lax.dynamic_slice_in_dim(
        gain_both, lax.axis_index("ctx") * gain_rows, gain_rows, 1
    )
    return (
        output[None],
        input_grad[None],
        gain_sums[0],
        gain_sums[1],
        shards[0],
        shards[1],
        shards[2],
        shards[3],
        shards[4],
        shards[5],
        shards[6],
    )


BF = jnp.bfloat16
F32 = jnp.float32
MESH = pl.DeviceIdType.MESH


def dot_nn(left, right):
    return lax.dot_general(left, right, (((1,), (0,)), ((), ())), preferred_element_type=F32)


def dot_nt(left, right):
    return lax.dot_general(left, right, (((1,), (1,)), ((), ())), preferred_element_type=F32)


def shift_lanes(field, amount):
    return pltpu.roll(field, amount, 1)


def widen(field, lanes):
    return jnp.concatenate(
        [field, jnp.zeros((field.shape[0], lanes - field.shape[1]), field.dtype)], axis=1
    )


def fast_kernel(
    n_dp,
    n_ctx,
    tok,
    cot,
    starts,
    gains,
    cos_ref,
    sin_ref,
    w_pack,
    w_gate,
    w_up,
    w_down,
    out_ref,
    ig_ref,
    gg_ref,
    g_pack_ref,
    g_gu_ref,
    g_down_ref,
    gb,
    wt,
    big,
    wd,
    wdz,
    na_ref,
    qt,
    kvb,
    sc,
    pp,
    rl,
    at,
    resid_ref,
    xb,
    cb,
    op,
    orecv,
    dn,
    drecv,
    dna,
    hb,
    dgu,
    xt,
    ct,
    gres,
    dat,
    rb,
    dkv,
    dkv_r,
    dkv_z,
    kvsum,
    gu_r,
    gu_z,
    gd,
    gd_r,
    gd_p,
    gd_z,
    g_r,
    g_p,
    g_z,
    nat,
    ggs,
    gg_p,
    gg_c,
    s_send,
    s_gain,
    s_a,
    s_ap,
    s_b,
    s_bz,
    s_bp,
    s_kv,
    s_gu,
    s_wd,
    s_wdz,
    s_x,
    s_c,
    s_o,
    s_d,
    s_dkv,
    s_gur,
    s_gdr,
    s_gdp,
    s_gdz,
    s_gr,
    s_gp,
    s_gz,
    s_ggp,
    s_ggc,
):
    n_z = n_ctx // 2
    rows_tok, model = tok.shape
    shard_rows = w_pack.shape[0]
    cq = model // n_dp
    ck = 96
    ffs = w_gate.shape[1]
    rf = w_down.shape[1]
    kvh = 6
    group = 3
    hs = HEAD_SIZE
    gl = group * rows_tok
    pack = w_pack.shape[1]
    d = lax.axis_index("dp")
    c = lax.axis_index("ctx")
    k = lax.rem(c, 2)
    z = c // 2
    mate = c + 1 - 2 * k
    my_down = pl.multiple_of(k * rf, 128)
    its_down = pl.multiple_of((1 - k) * rf, 128)
    big_sends = []
    pending = []
    counter = [0]

    def zc(i):
        return 2 * lax.rem(z + i, n_z) + k

    def dd_of(i):
        return lax.rem(d + i, n_dp)

    def rdma(src, dst, rsem, to_d, to_c):
        ssem = s_send.at[counter[0]]
        counter[0] += 1
        copy = pltpu.make_async_remote_copy(
            src_ref=src,
            dst_ref=dst,
            send_sem=ssem,
            recv_sem=rsem,
            device_id=(to_d, to_c),
            device_id_type=MESH,
        )
        copy.start()
        pending.append(copy)
        return copy

    def arrived(dst, rsem):
        pltpu.make_async_remote_copy(
            src_ref=dst,
            dst_ref=dst,
            send_sem=s_send.at[0],
            recv_sem=rsem,
            device_id=(d, mate),
            device_id_type=MESH,
        ).wait_recv()

    wt[d, z, k] = w_pack[...]
    gb[c] = gains[...]
    la = pl.ds(0, 512)
    lb = pl.ds(512, pack - 512)
    for i in range(1, n_z):
        rdma(wt.at[d, z, k, :, la], wt.at[d, z, k, :, la], s_a.at[0, n_z - i], d, zc(i))
    for i in range(1, n_dp):
        rdma(wt.at[d, z, k, :, la], wt.at[d, z, k, :, la], s_a.at[n_dp - i, 0], dd_of(i), c)
    for i in range(1, n_ctx):
        rdma(gb.at[c], gb.at[c], s_gain.at[n_ctx - i], d, lax.rem(c + i, n_ctx))
    big[k, 0, z] = w_gate[...]
    big[k, 1, z] = w_up[...]
    wdz[z] = w_down[...]
    own = n_dp - 1
    cb[own] = cot[...]

    def down_rows(e):
        return pl.ds(pl.multiple_of(e * cq, 32), cq)

    def spread_rows(e):
        for i in range(1, n_z):
            copy = rdma(big.at[k, e, z], big.at[k, e, z], s_gu.at[e, n_z - i], d, zc(i))
            big_sends.append(copy)

    for i in range(1, n_z):
        rdma(wt.at[d, z, k, :, lb], wt.at[d, z, k, :, lb], s_bz.at[n_z - i], d, zc(i))
    for i in range(1, n_z):
        rdma(wdz.at[z], wdz.at[z], s_wdz.at[n_z - i], d, zc(i))
    spread_rows(0)
    stream = tok[...].astype(F32)
    inv1 = lax.rsqrt(jnp.mean(stream * stream, axis=1, keepdims=True) + norm_eps)

    for q in (1, n_z - 1, 2):
        zq = lax.rem(z + q, n_z)
        arrived(wt.at[d, zq, k, :, la], s_a.at[0, q])
        for i in range(1, n_dp):
            rdma(
                wt.at[d, zq, k, :, la], wt.at[d, zq, k, :, la], s_a.at[n_dp - i, q], dd_of(i), c
            )
    rdma(wt.at[d, :, k, :, la], wt.at[d, :, k, :, la], s_ap.at[0], d, mate)
    for r in range(1, n_dp):
        dr = dd_of(r)
        for q in range(n_z):
            arrived(wt.at[dr, lax.rem(z + q, n_z), k, :, la], s_a.at[r, q])
        rdma(wt.at[dr, :, k, :, la], wt.at[dr, :, k, :, la], s_ap.at[r], d, mate)

    gain_all = jnp.zeros((8, model), F32)
    for i in range(1, n_ctx):
        arrived(gb.at[lax.rem(c + i, n_ctx)], s_gain.at[i])
    for e in range(n_ctx):
        piece = widen(gb[e], model)
        gain_all = gain_all + (piece if e == 0 else shift_lanes(piece, shard_rows * e))
    gain1 = gain_all[0:1]
    gain2 = gain_all[1:2]
    normed = (stream * inv1 * gain1).astype(BF)
    na_ref[...] = normed

    kt = kvsum
    for r in range(n_dp):
        arrived(wt.at[dd_of(r), :, 1 - k, :, la], s_ap.at[r])

    def project(e, _):
        w = wt[e, :, :, :, 0:512].reshape(model, 512)
        o = dot_nn(na_ref[...], w)
        o_t = jnp.transpose(o)
        at[pl.ds(pl.multiple_of(e * cq, 32), cq), :] = o_t[:cq]
        kt[pl.ds(pl.multiple_of(e * ck, 32), ck), :] = o_t[cq : cq + ck]
        kt[pl.ds(pl.multiple_of(model // 3 + e * ck, 32), ck), :] = o_t[cq + ck : cq + 2 * ck]
        return 0

    lax.fori_loop(0, n_dp, project, 0)
    cosine = cos_ref[...]
    sine = sin_ref[...]
    half = hs // 2

    def turn(first, second):
        return first * cosine - second * sine, second * cosine + first * sine

    def turn_back(first, second):
        return first * cosine + second * sine, second * cosine - first * sine

    kvw = model // 3
    for g in range(kvh):
        lo, hi = turn(kt[g * hs : g * hs + half], kt[g * hs + half : (g + 1) * hs])
        kvb[c, 128 * g : 128 * g + 64, :] = jnp.concatenate([lo, hi], axis=0).astype(BF)
        kvb[c, 128 * g + 64 : 128 * g + 128, :] = kt[kvw + g * hs : kvw + (g + 1) * hs].astype(BF)
    for i in range(1, n_z):
        rdma(kvb.at[c], kvb.at[c], s_kv.at[n_z - i], d, zc(i))
    rdma(kvb.at[c], kvb.at[c], s_kv.at[n_z], d, mate)
    spread_rows(1)
    for h in range(kvh * group):
        lo, hi = turn(at[h * hs : h * hs + half], at[h * hs + half : (h + 1) * hs])
        low = jnp.concatenate([lo, hi], axis=0).astype(BF)
        qt[h * hs : (h + 1) * hs, :] = (low.astype(F32) * 0.125).astype(BF)

    for q in range(1, n_z):
        zq = lax.rem(z + q, n_z)
        arrived(wt.at[d, zq, k, :, lb], s_bz.at[q])
    for i in range(1, n_dp):
        rdma(wt.at[d, :, k, :, lb], wt.at[d, :, k, :, lb], s_b.at[n_dp - i], dd_of(i), c)
    rdma(wt.at[d, :, k, :, lb], wt.at[d, :, k, :, lb], s_bp.at[0], d, mate)
    for q in range(1, n_z):
        arrived(wdz.at[lax.rem(z + q, n_z)], s_wdz.at[q])
    for i in range(1, n_dp):
        e = dd_of(i)
        rdma(wdz.at[e], wd.at[down_rows(d), pl.ds(my_down, rf)], s_wd.at[n_dp - i], e, c)
    wd[down_rows(d), pl.ds(my_down, rf)] = wdz[d]
    for i in range(1, n_dp):
        rdma(cb.at[own], cb.at[n_dp - i - 1], s_c.at[n_dp - i - 1], dd_of(i), c)
    for q in range(1, n_z):
        arrived(kvb.at[zc(q)], s_kv.at[q])
        rdma(kvb.at[zc(q)], kvb.at[zc(q)], s_kv.at[n_z + q], d, mate)
    for r in range(1, n_dp):
        dr = dd_of(r)
        arrived(wt.at[dr, :, k, :, lb], s_b.at[r])
        rdma(wt.at[dr, :, k, :, lb], wt.at[dr, :, k, :, lb], s_bp.at[r], d, mate)
    for q in range(n_z):
        arrived(kvb.at[2 * lax.rem(z + q, n_z) + 1 - k], s_kv.at[n_z + q])

    tpos = c * rows_tok + lax.broadcasted_iota(jnp.int32, (1, rows_tok), 1)
    lim = tpos
    for p in range(PICS):
        s_p = starts[0, p]
        lim = jnp.where((tpos >= s_p) & (tpos < s_p + PIC), jnp.maximum(lim, s_p + PIC - 1), lim)
    lim3 = jnp.concatenate([lim] * group, axis=1)

    def heads_of(ref, g):
        return jnp.concatenate(
            [
                ref[pl.ds(pl.multiple_of(g * group * hs + hs * j, hs), hs), :]
                for j in range(group)
            ],
            axis=1,
        )

    def attend(g, _):
        q_t = heads_of(qt, g)
        q_z = jnp.concatenate([q_t, jnp.zeros_like(q_t)], axis=0)
        k0 = pl.multiple_of(g * 128, 128)
        most = jnp.full((1, gl), -1e30, F32)
        for b in range(n_ctx):
            kv = jnp.transpose(kvb[b, pl.ds(k0, 128), :])
            s = dot_nn(kv, q_z)
            kpos = b * rows_tok + lax.broadcasted_iota(jnp.int32, (rows_tok, gl), 0)
            s = jnp.where(kpos <= lim3, s, -1e30)
            sc[b * rows_tok : (b + 1) * rows_tok, :] = s
            most = jnp.maximum(most, jnp.max(s, axis=0, keepdims=True))
        total = jnp.zeros((1, gl), F32)
        o_t = jnp.zeros((hs, gl), F32)
        for b in range(n_ctx):
            p = jnp.exp(sc[b * rows_tok : (b + 1) * rows_tok, :] - most)
            p_low = p.astype(BF)
            pp[g, b * rows_tok : (b + 1) * rows_tok, :] = p_low
            total = total + jnp.sum(p, axis=0, keepdims=True)
            o_t = o_t + dot_nn(kvb[b, pl.ds(pl.multiple_of(k0 + hs, hs), hs), :], p_low)
        inv = 1.0 / total
        rl[g] = jnp.broadcast_to(inv, (8, gl))
        o_t = o_t * inv
        for j in range(group):
            at[pl.ds(pl.multiple_of(g * group * hs + hs * j, hs), hs), :] = o_t[
                :, rows_tok * j : rows_tok * (j + 1)
            ]
        return 0

    lax.fori_loop(0, kvh, attend, 0)

    for r in range(1, n_dp):
        arrived(wd.at[down_rows(dd_of(r)), pl.ds(my_down, rf)], s_wd.at[r])
    rdma(wd.at[:, pl.ds(my_down, rf)], wd.at[:, pl.ds(my_down, rf)], s_wd.at[0], d, mate)
    for e in range(2):
        copy = rdma(big.at[k, e, z], big.at[k, e, z], s_gu.at[e, n_z], d, mate)
        big_sends.append(copy)
        for q in range(1, n_z):
            zq = lax.rem(z + q, n_z)
            arrived(big.at[k, e, zq], s_gu.at[e, q])
            copy = rdma(big.at[k, e, zq], big.at[k, e, zq], s_gu.at[e, n_z + q], d, mate)
            big_sends.append(copy)

    att_t = at[...].astype(BF)
    nat[:, 0:rows_tok] = jnp.transpose(na_ref[...])
    nat[:, rows_tok : 2 * rows_tok] = att_t
    na_ref[...] = jnp.transpose(att_t)
    resid_ref[...] = tok[...].astype(F32)
    for r in range(n_dp):
        arrived(wt.at[dd_of(r), :, 1 - k, :, lb], s_bp.at[r])
    lead = 2 * ck + cq - 384

    def out_block(e, _):
        w = wt[e, :, :, :, 384:pack].reshape(model, pack - 384)
        o = dot_nn(na_ref[...], w)
        lane = lax.broadcasted_iota(jnp.int32, o.shape, 1)
        o = widen(jnp.where(lane >= lead, o, 0.0), model)
        resid_ref[...] += shift_lanes(o, lax.rem(e * cq + model - lead, model))
        return 0

    lax.fori_loop(0, n_dp, out_block, 0)
    resid = resid_ref[...]
    inv2 = lax.rsqrt(jnp.mean(resid * resid, axis=1, keepdims=True) + norm_eps)
    xb[own] = (resid * inv2 * gain2).astype(BF)
    for i in range(1, n_dp):
        rdma(xb.at[own], xb.at[n_dp - i - 1], s_x.at[n_dp - i - 1], dd_of(i), c)
    xt[:, own * rows_tok :] = jnp.transpose(xb[own])
    for p in range(n_dp - 1):
        arrived(cb.at[p], s_c.at[p])
    for p in range(n_dp):
        ct[:, p * rows_tok : (p + 1) * rows_tok] = jnp.transpose(cb[p])
    for e in range(2):
        for q in range(n_z):
            arrived(big.at[1 - k, e, lax.rem(z + q, n_z)], s_gu.at[e, n_z + q])
    arrived(wd.at[:, pl.ds(its_down, rf)], s_wd.at[0])
    for p in range(n_dp - 1):
        arrived(xb.at[p], s_x.at[p])

    nc = 256

    def weight_cols(e, n0):
        return jnp.concatenate(
            [big[b % 2, e, b // 2, :, pl.ds(n0, nc)] for b in range(n_ctx)], axis=0
        )

    for hf in range(n_dp // 2):
        t0 = 2 * hf
        r0 = t0 * rows_tok
        rh = 2 * rows_tok
        dna[...] = jnp.zeros_like(dna)

        def cols(n, _):
            n0 = pl.multiple_of(n * nc, nc)
            n1 = pl.multiple_of(n * nc + ffs, nc)
            x = xb[t0 : t0 + 2].reshape(rh, model)
            w_g = weight_cols(0, n0)
            w_u = weight_cols(1, n0)
            g = dot_nn(x, w_g)
            u = dot_nn(x, w_u)
            dh = dot_nn(cb[t0 : t0 + 2].reshape(rh, model), wd[:, pl.ds(n0, nc)])
            sg = jax.nn.sigmoid(g)
            si = g * sg
            hb[r0 : r0 + rh, pl.ds(n0, nc)] = (si * u).astype(BF)
            dg = (dh * u * sg * (1.0 + g * (1.0 - sg))).astype(BF)
            du = (dh * si).astype(BF)
            dgu[r0 : r0 + rh, pl.ds(n0, nc)] = dg
            dgu[r0 : r0 + rh, pl.ds(n1, nc)] = du
            dna[...] += dot_nt(dg, w_g) + dot_nt(du, w_u)
            return 0

        lax.fori_loop(0, ffs // nc, cols, 0)
        dn[t0 : t0 + 2] = dna[...].astype(BF).reshape(2, rows_tok, model)
        for p in (t0, t0 + 1):
            if p != own:
                there = n_dp - p - 2
                rdma(dn.at[p], drecv.at[there], s_d.at[there], dd_of(p + 1), c)
        y = dot_nt(hb[r0 : r0 + rh, :], wd[...])
        op[t0 : t0 + 2] = y.astype(BF).reshape(2, rows_tok, model)
        for p in (t0, t0 + 1):
            if p != own:
                there = n_dp - p - 2
                rdma(op.at[p], orecv.at[there], s_o.at[there], dd_of(p + 1), c)

    for p in range(n_dp - 1):
        xt[:, p * rows_tok : (p + 1) * rows_tok] = jnp.transpose(xb[p])
    for e in range(2):

        def gu_cols(n, _):
            n0 = pl.multiple_of(n * nc, nc)
            n1 = pl.multiple_of(n * nc + e * ffs, nc)
            r = dot_nn(xt[...], dgu[:, pl.ds(n1, nc)]).astype(BF)
            for b in range(n_ctx):
                big[b % 2, 2 + e, b // 2, :, pl.ds(n0, nc)] = r[
                    shard_rows * b : shard_rows * (b + 1)
                ]
            return 0

        lax.fori_loop(0, ffs // nc, gu_cols, 0)
    big_sends.append(rdma(big.at[1 - k, 2:4], gu_r, s_gur.at[0], d, mate))

    def gd_cols(j, _):
        r = dot_nn(ct[...], hb[:, pl.ds(pl.multiple_of(j * rf, 128), rf)]).astype(BF)
        for e in range(n_dp):
            gd[j, e] = r[cq * e : cq * (e + 1)]
        return 0

    lax.fori_loop(0, 2, gd_cols, 0)
    rdma(gd.at[1 - k], gd_r, s_gdr.at[0], d, mate)

    for p in range(n_dp - 1):
        arrived(drecv.at[p], s_d.at[p])
    d_nm = dna[rows_tok : 2 * rows_tok, :]
    for p in range(n_dp - 1):
        d_nm = d_nm + drecv[p].astype(F32)

    def norm_out(inputs, inverse, gain_vec, upstream):
        scaled = gain_vec * upstream
        return inverse * scaled - inputs * inverse * inverse * inverse * jnp.mean(
            scaled * inputs, axis=1, keepdims=True
        )

    resid = resid_ref[...]
    ggs[1:2, :] = jnp.sum(d_nm * resid * inv2, axis=0, keepdims=True)
    d_res = cot[...].astype(F32) + norm_out(resid, inv2, gain2, d_nm)
    gres[...] = d_res
    d_low = d_res.astype(BF).astype(F32)
    o0 = 2 * ck + cq
    for e in range(n_dp):
        t = shift_lanes(d_low, (o0 - cq * e) % model)[:, :pack]
        lane = lax.broadcasted_iota(jnp.int32, t.shape, 1)
        rb[e, rows_tok : 2 * rows_tok, :] = jnp.where(lane >= o0, t, 0.0).astype(BF)
    dna[...] = jnp.zeros_like(dna)

    def att_block(e, _):
        w = wt[e, :, :, :, 384:pack].reshape(model, pack - 384)
        dna[0:rows_tok, :] += dot_nt(rb[e, rows_tok : 2 * rows_tok, 384:pack], w)
        return 0

    lax.fori_loop(0, n_dp, att_block, 0)
    dat[...] = jnp.transpose(dna[0:rows_tok, :].astype(BF))

    arrived(gu_r, s_gur.at[0])

    def gu_sum(n, _):
        e = n // n_z
        j = lax.rem(n, n_z)
        gu_r[e, j] = (gu_r[e, j].astype(F32) + big[k, 2 + e, j].astype(F32)).astype(BF)
        return 0

    lax.fori_loop(0, 2 * n_z, gu_sum, 0)
    for i in range(1, n_z):
        there = n_z - i - 1
        rdma(
            gu_r.at[:, lax.rem(z + i, n_z)], gu_z.at[there], s_gur.at[there + 1], d, zc(i)
        )
    arrived(gd_r, s_gdr.at[0])

    def gd_sum(e, _):
        gd_r[e] = (gd_r[e].astype(F32) + gd[k, e].astype(F32)).astype(BF)
        return 0

    lax.fori_loop(0, n_dp, gd_sum, 0)
    for i in range(1, n_dp):
        rdma(gd_r.at[dd_of(i)], gd_p.at[d], s_gdp.at[n_dp - i], dd_of(i), c)
    gd_p[d] = gd_r[d]

    for copy in big_sends:
        copy.wait_send()
    pending[:] = [copy for copy in pending if all(copy is not other for other in big_sends)]

    def store_pack(e, n0, t):
        for b in range(n_ctx):
            big[b % 2, e, b // 2, :, pl.ds(n0, nc)] = t[shard_rows * b : shard_rows * (b + 1)]

    def chip_sum(r, s, lanes):
        e = dd_of(r)
        arrived(g_r.at[e, :, :, lanes], s_gr.at[s, r])

        def one(j, _):
            mine = big[k, e, j, :, lanes].astype(F32)
            g_r[e, j, :, lanes] = (g_r[e, j, :, lanes].astype(F32) + mine).astype(BF)
            return 0

        lax.fori_loop(0, n_z, one, 0)
        return e

    def to_plane(s, lanes):
        for r in range(1, n_dp):
            e = chip_sum(r, s, lanes)
            there = n_dp - r - 1
            rdma(
                g_r.at[e, :, :, lanes], g_p.at[there, :, :, lanes], s_gp.at[s, there], e, c
            )

    def plane_sum(j, lanes):
        t = g_r[d, j, :, lanes].astype(F32)
        for p in range(n_dp - 1):
            t = t + g_p[p, j, :, lanes].astype(F32)
        return t

    def to_z(s, lanes):
        for p in range(n_dp - 1):
            arrived(g_p.at[p, :, :, lanes], s_gp.at[s, p])
        for i in range(1, n_z):
            zq = lax.rem(z + i, n_z)
            there = n_z - i - 1
            g_r[d, zq, :, lanes] = plane_sum(zq, lanes).astype(BF)
            rdma(
                g_r.at[d, zq, :, lanes], g_z.at[there, :, lanes], s_gz.at[s, there], d, zc(i)
            )
        g_pack_ref[:, lanes] = plane_sum(z, lanes)

    def last_sum(s, lanes):
        for i in range(n_z - 1):
            arrived(g_z.at[i, :, lanes], s_gz.at[s, i])
        t = g_pack_ref[:, lanes]
        for i in range(n_z - 1):
            t = t + g_z[i, :, lanes].astype(F32)
        g_pack_ref[:, lanes] = t

    for r in (1, 2, 3, 0):
        e = dd_of(r)
        t = dot_nn(
            nat[:, rows_tok : 2 * rows_tok], rb[e, rows_tok : 2 * rows_tok, 512:pack]
        ).astype(BF)
        store_pack(e, 512, t)
        rdma(big.at[1 - k, e, :, :, lb], g_r.at[e, :, :, lb], s_gr.at[1, r], d, mate)
    to_plane(1, lb)

    def attend_back(g, _):
        q_t = heads_of(qt, g)
        a_t = heads_of(dat, g)
        o_t = heads_of(at, g)
        none = jnp.zeros_like(q_t)
        inv = rl[g][0:1]
        delta = jnp.sum(a_t.astype(F32) * o_t, axis=0, keepdims=True) * inv
        a_z = jnp.concatenate([none, a_t], axis=0)
        a_inv = (a_t.astype(F32) * inv).astype(BF)
        q2 = jnp.transpose(jnp.concatenate([q_t, none], axis=0))
        a2 = jnp.transpose(jnp.concatenate([none, a_inv], axis=0))
        k0 = pl.multiple_of(g * 128, 128)
        dq = jnp.zeros((hs, gl), F32)
        for b in range(n_ctx):
            kv_t = kvb[b, pl.ds(k0, 128), :]
            dp = dot_nn(jnp.transpose(kv_t), a_z)
            p_low = pp[g, b * rows_tok : (b + 1) * rows_tok, :]
            ds = (p_low.astype(F32) * (dp * inv - delta)).astype(BF)
            dq = dq + dot_nn(kv_t[:hs], ds)
            both = dot_nn(ds, q2) + dot_nn(p_low, a2)
            dkv[b % 2, b // 2, pl.ds(k0, 128), :] = jnp.transpose(both).astype(BF)
        dq = dq * 0.125
        for j in range(group):
            at[pl.ds(pl.multiple_of(g * group * hs + hs * j, hs), hs), :] = dq[
                :, rows_tok * j : rows_tok * (j + 1)
            ]
        return 0

    lax.fori_loop(0, kvh, attend_back, 0)
    rdma(dkv.at[1 - k], dkv_r, s_dkv.at[0], d, mate)
    for h in range(kvh * group):
        lo, hi = turn_back(at[h * hs : h * hs + half], at[h * hs + half : (h + 1) * hs])
        qt[h * hs : (h + 1) * hs, :] = jnp.concatenate([lo, hi], axis=0).astype(BF)
    arrived(dkv_r, s_dkv.at[0])

    def kv_sum(j, _):
        dkv_r[j] = (dkv_r[j].astype(F32) + dkv[k, j].astype(F32)).astype(BF)
        return 0

    lax.fori_loop(0, n_z, kv_sum, 0)
    for i in range(1, n_z):
        there = n_z - i - 1
        rdma(dkv_r.at[lax.rem(z + i, n_z)], dkv_z.at[there], s_dkv.at[there + 1], d, zc(i))
    chip_sum(0, 1, lb)
    to_z(1, lb)
    for r in range(1, n_dp):
        arrived(gd_p.at[dd_of(r)], s_gdp.at[r])
    for i in range(1, n_z):
        there = n_z - i - 1
        rdma(gd_p.at[lax.rem(z + i, n_z)], gd_z.at[there], s_gdz.at[there], d, zc(i))

    for p in range(n_dp - 1):
        arrived(orecv.at[p], s_o.at[p])
    y_all = resid_ref[...] + op[own].astype(F32)
    for p in range(n_dp - 1):
        y_all = y_all + orecv[p].astype(F32)
    out_ref[...] = y_all.astype(BF)

    for i in range(n_z - 1):
        arrived(dkv_z.at[i], s_dkv.at[i + 1])
    kv_total = dkv_r[z].astype(F32)
    for i in range(n_z - 1):
        kv_total = kv_total + dkv_z[i].astype(F32)
    kvsum[...] = kv_total
    for g in range(kvh):
        r = 128 * g
        lo, hi = turn_back(kvsum[r : r + half], kvsum[r + half : r + hs])
        at[g * hs : (g + 1) * hs, :] = jnp.concatenate([lo, hi], axis=0)
        at[kvw + g * hs : kvw + (g + 1) * hs, :] = kvsum[r + hs : r + 2 * hs]
    for e in range(n_dp):
        rows = jnp.concatenate(
            [
                qt[cq * e : cq * (e + 1)],
                at[ck * e : ck * (e + 1)].astype(BF),
                at[kvw + ck * e : kvw + ck * (e + 1)].astype(BF),
                jnp.zeros((512 - o0, rows_tok), BF),
            ],
            axis=0,
        )
        rb[e, 0:rows_tok, :] = widen(jnp.transpose(rows), pack)

    for r in (1, 2, 3, 0):
        e = dd_of(r)

        def pack_cols(n, _):
            n0 = pl.multiple_of(n * nc, nc)
            store_pack(e, n0, dot_nn(nat[...], rb[e, :, pl.ds(n0, nc)]).astype(BF))
            return 0

        lax.fori_loop(0, 512 // nc, pack_cols, 0)
        rdma(big.at[1 - k, e, :, :, la], g_r.at[e, :, :, la], s_gr.at[0, r], d, mate)

    to_plane(0, la)

    dna[...] = jnp.zeros_like(dna)

    def in_block(e, _):
        w = wt[e, :, :, :, 0:512].reshape(model, 512)
        dna[0:rows_tok, :] += dot_nt(rb[e, 0:rows_tok, 0:512], w)
        return 0

    lax.fori_loop(0, n_dp, in_block, 0)
    d_na = dna[0:rows_tok, :]
    stream = tok[...].astype(F32)
    ggs[0:1, :] = jnp.sum(d_na * stream * inv1, axis=0, keepdims=True)
    ig_ref[...] = gres[...] + norm_out(stream, inv1, gain1, d_na)
    for i in range(1, n_dp):
        there = n_dp - i - 1
        rdma(ggs, gg_p.at[there], s_ggp.at[there], dd_of(i), c)
    chip_sum(0, 0, la)
    for p in range(n_dp - 1):
        arrived(gg_p.at[p], s_ggp.at[p])
    gg_all = ggs[...]
    for p in range(n_dp - 1):
        gg_all = gg_all + gg_p[p]
    gg_c[0] = gg_all
    for i in range(1, n_ctx):
        rdma(gg_c.at[0], gg_c.at[n_ctx - i], s_ggc.at[n_ctx - i], d, lax.rem(c + i, n_ctx))
    for i in range(n_z - 1):
        arrived(gu_z.at[i], s_gur.at[i + 1])
    for e in range(2):
        t = gu_r[e, z].astype(F32)
        for i in range(n_z - 1):
            t = t + gu_z[i, e].astype(F32)
        g_gu_ref[e] = t
    for i in range(n_z - 1):
        arrived(gd_z.at[i], s_gdz.at[i])
    t = gd_p[z].astype(F32)
    for i in range(n_z - 1):
        t = t + gd_z[i].astype(F32)
    g_down_ref[...] = t
    last_sum(1, lb)
    to_z(0, la)
    for i in range(1, n_ctx):
        arrived(gg_c.at[i], s_ggc.at[i])
    gg_tot = gg_c[0]
    for i in range(1, n_ctx):
        gg_tot = gg_tot + gg_c[i]
    gg_ref[...] = shift_lanes(gg_tot, lax.rem(model - shard_rows * c, model))[:, :256]
    last_sum(0, la)
    for copy in pending:
        copy.wait_send()
def fast_body(
    n_dp,
    n_ctx,
    tokens,
    starts,
    gain_attn,
    gain_mlp,
    w_query,
    w_key,
    w_value,
    w_out,
    w_gate,
    w_up,
    w_down,
    cotangent,
):
    n_z = n_ctx // 2
    rows_tok, model = tokens.shape[1:]
    sr = w_query.shape[0]
    rf, cd = w_down.shape
    ffs = w_gate.shape[1]
    cq = w_query.shape[1]
    ck = w_key.shape[1]
    pack = 2 * (cq + ck)
    length = rows_tok * n_ctx
    gl = 3 * rows_tok
    packed = jnp.concatenate([w_query, w_key, w_value, w_out], axis=1)
    down = jnp.transpose(w_down)
    gains = jnp.pad(
        jnp.stack([gain_attn, gain_mlp]).astype(jnp.float32), ((0, 6), (0, 256 - sr))
    )
    half = HEAD_SIZE // 2
    positions = lax.axis_index("ctx") * rows_tok + jnp.arange(rows_tok)
    freqs = 10000.0 ** (-jnp.arange(half).astype(jnp.float32) / half)
    angles = freqs[:, None] * positions.astype(jnp.float32)[None, :]
    vm = pl.BlockSpec(memory_space=pltpu.VMEM)
    dma = pltpu.SemaphoreType.DMA
    n = n_dp - 1
    m = n_z - 1
    scratch = [
        pltpu.VMEM((n_ctx, 8, 256), F32),
        pltpu.VMEM((n_dp, n_z, 2, sr, pack), BF),
        pltpu.VMEM((2, n_dp, n_z, sr, ffs), BF),
        pltpu.VMEM((model, 2 * rf), BF),
        pltpu.VMEM((n_z, cd, rf), BF),
        pltpu.VMEM((rows_tok, model), BF),
        pltpu.VMEM((model, rows_tok), BF),
        pltpu.VMEM((n_ctx, 2 * model // 3, rows_tok), BF),
        pltpu.VMEM((length, gl), F32),
        pltpu.VMEM((6, length, gl), BF),
        pltpu.VMEM((6, 8, gl), F32),
        pltpu.VMEM((model, rows_tok), F32),
        pltpu.VMEM((rows_tok, model), F32),
        pltpu.VMEM((n_dp, rows_tok, model), BF),
        pltpu.VMEM((n_dp, rows_tok, model), BF),
        pltpu.VMEM((n_dp, rows_tok, model), BF),
        pltpu.VMEM((n, rows_tok, model), BF),
        pltpu.VMEM((n_dp, rows_tok, model), BF),
        pltpu.VMEM((n, rows_tok, model), BF),
        pltpu.VMEM((2 * rows_tok, model), F32),
        pltpu.VMEM((n_dp * rows_tok, ffs), BF),
        pltpu.VMEM((n_dp * rows_tok, 2 * ffs), BF),
        pltpu.VMEM((model, n_dp * rows_tok), BF),
        pltpu.VMEM((model, n_dp * rows_tok), BF),
        pltpu.VMEM((rows_tok, model), F32),
        pltpu.VMEM((model, rows_tok), BF),
        pltpu.VMEM((n_dp, 2 * rows_tok, pack), BF),
        pltpu.VMEM((2, n_z, 2 * model // 3, rows_tok), BF),
        pltpu.VMEM((n_z, 2 * model // 3, rows_tok), BF),
        pltpu.VMEM((m, 2 * model // 3, rows_tok), BF),
        pltpu.VMEM((2 * model // 3, rows_tok), F32),
        pltpu.VMEM((2, n_z, sr, ffs), BF),
        pltpu.VMEM((m, 2, sr, ffs), BF),
        pltpu.VMEM((2, n_dp, cd, rf), BF),
        pltpu.VMEM((n_dp, cd, rf), BF),
        pltpu.VMEM((n_dp, cd, rf), BF),
        pltpu.VMEM((m, cd, rf), BF),
        pltpu.VMEM((n_dp, n_z, sr, pack), BF),
        pltpu.VMEM((n, n_z, sr, pack), BF),
        pltpu.VMEM((m, sr, pack), BF),
        pltpu.VMEM((model, 2 * rows_tok), BF),
        pltpu.VMEM((8, model), F32),
        pltpu.VMEM((n, 8, model), F32),
        pltpu.VMEM((n_ctx, 8, model), F32),
        dma((150,)),
        dma((n_ctx,)),
        dma((n_dp, n_z)),
        dma((n_dp,)),
        dma((n_dp,)),
        dma((n_z,)),
        dma((n_dp,)),
        dma((2 * n_z,)),
        dma((2, 2 * n_z)),
        dma((n_dp,)),
        dma((n_z,)),
        dma((n,)),
        dma((n,)),
        dma((n,)),
        dma((n,)),
        dma((n_z,)),
        dma((n_z,)),
        dma((1,)),
        dma((n_dp,)),
        dma((m,)),
        dma((2, n_dp)),
        dma((2, n)),
        dma((2, m)),
        dma((n,)),
        dma((n_ctx,)),
    ]
    out, ig, gg, g_pack, g_gu, g_down = pl.pallas_call(
        functools.partial(fast_kernel, n_dp, n_ctx),
        out_shape=(
            jax.ShapeDtypeStruct((rows_tok, model), BF),
            jax.ShapeDtypeStruct((rows_tok, model), F32),
            jax.ShapeDtypeStruct((8, 256), F32),
            jax.ShapeDtypeStruct((sr, pack), F32),
            jax.ShapeDtypeStruct((2, sr, ffs), F32),
            jax.ShapeDtypeStruct((cd, rf), F32),
        ),
        in_specs=[vm, vm, pl.BlockSpec(memory_space=pltpu.SMEM)] + [vm] * 7,
        out_specs=(vm,) * 6,
        scratch_shapes=scratch,
        compiler_params=pltpu.CompilerParams(
            has_side_effects=True, vmem_limit_bytes=67043328
        ),
        name="layer",
    )(
        tokens[0],
        cotangent[0],
        starts,
        gains,
        jnp.cos(angles),
        jnp.sin(angles),
        packed,
        w_gate,
        w_up,
        down,
    )
    return (
        out[None],
        ig[None],
        gg[0, :sr],
        gg[1, :sr],
        g_pack[:, :cq],
        g_pack[:, cq : cq + ck],
        g_pack[:, cq + ck : cq + 2 * ck],
        g_pack[:, cq + 2 * ck :],
        g_gu[0],
        g_gu[1],
        jnp.transpose(g_down),
    )


def solution(mesh):
    n_dp = mesh.shape["dp"]
    n_ctx = mesh.shape["ctx"]

    def choose(tokens, *rest):
        fits = n_dp == 4 and n_ctx == 2 * n_dp and tokens.shape[1:] == (128, 1152)
        if fits:
            return fast_body(n_dp, n_ctx, tokens, *rest)
        return body(tokens, *rest)

    return jax.shard_map(
        choose,
        mesh=mesh,
        in_specs=(
            P("dp", "ctx", None),
            P("dp", None),
            P("ctx"),
            P("ctx"),
            P("ctx", "dp"),
            P("ctx", "dp"),
            P("ctx", "dp"),
            P("ctx", "dp"),
            P("ctx", "dp"),
            P("ctx", "dp"),
            P("ctx", "dp"),
            P("dp", "ctx", None),
        ),
        out_specs=(
            P("dp", "ctx", None),
            P("dp", "ctx", None),
            P("ctx"),
            P("ctx"),
            P("ctx", "dp"),
            P("ctx", "dp"),
            P("ctx", "dp"),
            P("ctx", "dp"),
            P("ctx", "dp"),
            P("ctx", "dp"),
            P("ctx", "dp"),
        ),
        check_vma=False,
    )
```

```python
import functools

import jax
import jax.numpy as jnp
from jax import lax
from jax.experimental import pallas as pl
from jax.experimental.pallas import tpu as pltpu
from jax.sharding import PartitionSpec as P

HEAD_SIZE = 64
PIC = 256
PICS = 4


norm_eps = 1e-05


def rotary_embedding(field, token_positions):
    half = field.shape[-1] // 2
    freqs = 10000.0 ** (-jnp.arange(half).astype(jnp.float32) / half)
    angles = token_positions.astype(jnp.float32)[:, None] * freqs[None, :]
    cosine = jnp.cos(angles)[:, None, :]
    sine = jnp.sin(angles)[:, None, :]
    first = field[..., :half]
    second = field[..., half:]
    return jnp.concatenate(
        [first * cosine - second * sine, second * cosine + first * sine], axis=-1
    )


def rotary_back(field, token_positions):
    half = field.shape[-1] // 2
    freqs = 10000.0 ** (-jnp.arange(half).astype(jnp.float32) / half)
    angles = token_positions.astype(jnp.float32)[:, None] * freqs[None, :]
    cosine = jnp.cos(angles)[:, None, :]
    sine = jnp.sin(angles)[:, None, :]
    first = field[..., :half]
    second = field[..., half:]
    return jnp.concatenate(
        [first * cosine + second * sine, second * cosine - first * sine], axis=-1
    )


def piece_ids(token_positions, seq_starts):
    inside = (token_positions[:, None] >= seq_starts[None, :]) & (
        token_positions[:, None] < seq_starts[None, :] + PIC
    )
    labels = jnp.arange(1, PICS + 1)
    return jnp.sum(jnp.where(inside, labels[None, :], 0), axis=1) - 1


def norm_back(inputs, inverse, gain_vec, upstream):
    scaled = gain_vec * upstream
    return inverse * scaled - inputs * inverse**3 * jnp.mean(
        scaled * inputs, axis=-1, keepdims=True
    )


def fetch_weights(gain_attn, gain_mlp, w_query, w_key, w_value, w_out, w_gate, w_up, w_down):
    packed = jnp.concatenate([w_query, w_key, w_value, w_out], axis=1)
    gains = lax.all_gather(jnp.stack([gain_attn, gain_mlp]), "ctx", axis=1, tiled=True)
    packed = lax.all_gather(packed, ("dp", "ctx"), axis=0, tiled=True)
    packed = packed.reshape(lax.axis_size("dp"), -1, packed.shape[1])
    gate_up = lax.all_gather(jnp.concatenate([w_gate, w_up], axis=1), "ctx", axis=0, tiled=True)
    down = lax.all_gather(w_down, "ctx", axis=0, tiled=True)
    cuts = []
    first = 0
    for shard in (w_query, w_key, w_value, w_out):
        part = packed[:, :, first : first + shard.shape[1]]
        cuts.append(jnp.transpose(part, (1, 0, 2)).reshape(part.shape[1], -1))
        first += shard.shape[1]
    ff = w_gate.shape[1]
    return (gains[0], gains[1], *cuts, gate_up[:, :ff], gate_up[:, ff:], down)


def gather_keys(key_rot, value_low):
    return (
        lax.all_gather(key_rot, "ctx", axis=0, tiled=True),
        lax.all_gather(value_low, "ctx", axis=0, tiled=True),
    )


def delta_of(grad_rows, attended_rows):
    return jnp.transpose(jnp.sum(grad_rows.astype(jnp.float32) * attended_rows, axis=-1), (1, 2, 0))


def as_rows(stat):
    return jnp.transpose(stat, (2, 0, 1)).reshape(stat.shape[2], -1)


def body(
    tokens,
    starts,
    gain_attn,
    gain_mlp,
    w_query,
    w_key,
    w_value,
    w_out,
    w_gate,
    w_up,
    w_down,
    cotangent,
):
    tok_count = tokens.shape[1]
    length = tok_count * lax.axis_size("ctx")
    span = min(512, length)
    n_blocks = length // span
    query_pos = lax.axis_index("ctx") * tok_count + jnp.arange(tok_count)
    seq_starts = starts[0]
    labels_all = piece_ids(jnp.arange(length), seq_starts)

    def reach_of(token_positions):
        inside = (token_positions[:, None] >= seq_starts[None, :]) & (
            token_positions[:, None] < seq_starts[None, :] + PIC
        )
        return jnp.maximum(
            token_positions[-1], jnp.max(jnp.where(inside, seq_starts[None, :] + PIC - 1, -1))
        )

    gathered = fetch_weights(
        gain_attn, gain_mlp, w_query, w_key, w_value, w_out, w_gate, w_up, w_down
    )
    (
        gain_first,
        gain_second,
        mat_query,
        key_projection,
        value_projection,
        mat_out,
        mat_gate,
        mat_up,
        mat_down,
    ) = gathered
    heads_kv = key_projection.shape[1] // HEAD_SIZE
    group_size = mat_query.shape[1] // key_projection.shape[1]
    score_scale = HEAD_SIZE ** (-0.5)
    gain_one = gain_first.astype(jnp.float32)
    gain_two = gain_second.astype(jnp.float32)
    stream = tokens[0].astype(jnp.float32)
    inv_one = lax.rsqrt(jnp.mean(stream * stream, axis=-1, keepdims=True) + norm_eps)
    attention_normed = (stream * inv_one * gain_one).astype(jnp.bfloat16)
    query_unrotated = jnp.dot(attention_normed, mat_query, preferred_element_type=jnp.float32)
    key_unrotated = jnp.dot(attention_normed, key_projection, preferred_element_type=jnp.float32)
    v_pre = jnp.dot(attention_normed, value_projection, preferred_element_type=jnp.float32)
    query_vectors = (
        rotary_embedding(query_unrotated.reshape(tok_count, -1, HEAD_SIZE), query_pos)
        .astype(jnp.bfloat16)
        .reshape(tok_count, -1)
    )
    key_rot = (
        rotary_embedding(key_unrotated.reshape(tok_count, heads_kv, HEAD_SIZE), query_pos)
        .astype(jnp.bfloat16)
        .reshape(tok_count, -1)
    )
    value_low = v_pre.astype(jnp.bfloat16)
    key_all, value_all = gather_keys(key_rot, value_low)

    def key_block(source, block_index):
        return lax.dynamic_slice_in_dim(source, block_index * span, span, 0).reshape(
            span, heads_kv, HEAD_SIZE
        )

    def scores_at(block_index, key_piece, query_set, row_pos, row_lab):
        first_key = block_index * span
        key_pos = first_key + jnp.arange(span)
        key_lab = lax.dynamic_slice_in_dim(labels_all, first_key, span, 0)
        raw = (
            jnp.einsum("qhgd,khd->hgqk", query_set, key_piece, preferred_element_type=jnp.float32)
            * score_scale
        )
        allowed = (key_pos[None, :] <= row_pos[:, None]) | (
            row_lab[:, None] == key_lab[None, :]
        ) & (row_lab[:, None] >= 0)
        return jnp.where(allowed[None, None], raw, -1e30)

    keys_now = key_all
    values_now = value_all
    rows = query_vectors.shape[0]
    query_set = query_vectors.reshape(rows, heads_kv, group_size, HEAD_SIZE)
    row_lab = piece_ids(query_pos, seq_starts)
    reach = reach_of(query_pos)

    def lse_step(running, block_index):

        def lse_live(pair_now):
            most_now, sum_now = pair_now
            masked = scores_at(
                block_index, key_block(keys_now, block_index), query_set, query_pos, row_lab
            )
            most_new = jnp.maximum(most_now, jnp.max(masked, axis=-1))
            sum_new = sum_now * jnp.exp(most_now - most_new) + jnp.sum(
                jnp.exp(masked - most_new[..., None]), axis=-1
            )
            return (most_new, sum_new)

        return (
            lax.cond(block_index * span <= reach, lse_live, lambda pair_now: pair_now, running),
            None,
        )

    start_pair = (
        jnp.full((heads_kv, group_size, rows), -1e30, jnp.float32),
        jnp.zeros((heads_kv, group_size, rows), jnp.float32),
    )
    (most_all, sum_all), _ = lax.scan(lse_step, start_pair, jnp.arange(n_blocks))
    log_norm = most_all + jnp.log(sum_all)

    def out_step(running, block_index):

        def out_live(acc_now):
            masked = scores_at(
                block_index, key_block(keys_now, block_index), query_set, query_pos, row_lab
            )
            chances = jnp.exp(masked - log_norm[..., None]).astype(jnp.bfloat16)
            return acc_now + jnp.einsum(
                "hgqk,khd->qhgd",
                chances,
                key_block(values_now, block_index),
                preferred_element_type=jnp.float32,
            )

        return (
            lax.cond(block_index * span <= reach, out_live, lambda acc_now: acc_now, running),
            None,
        )

    attended_set, _ = lax.scan(
        out_step,
        jnp.zeros((rows, heads_kv, group_size, HEAD_SIZE), jnp.float32),
        jnp.arange(n_blocks),
    )
    att_low = attended_set.reshape(tok_count, -1).astype(jnp.bfloat16)
    resid = stream + jnp.dot(att_low, mat_out, preferred_element_type=jnp.float32)
    inv_two = lax.rsqrt(jnp.mean(resid * resid, axis=-1, keepdims=True) + norm_eps)
    normed_m = (resid * inv_two * gain_two).astype(jnp.bfloat16)
    width = mat_down.shape[1]
    group_normed = lax.all_gather(normed_m, "dp", axis=0, tiled=True)
    grad_low = cotangent[0]
    group_cot = lax.all_gather(grad_low, "dp", axis=0, tiled=True)
    cot_cols = lax.dynamic_slice_in_dim(group_cot, lax.axis_index("dp") * width, width, 1)
    grad_hidden_part = jnp.einsum(
        "td,fd->tf", cot_cols, mat_down, preferred_element_type=jnp.float32
    ).astype(jnp.bfloat16)
    grad_hidden = lax.psum_scatter(
        grad_hidden_part, "dp", scatter_dimension=1, tiled=True
    ).astype(jnp.float32)
    gate_pre = jnp.dot(group_normed, mat_gate, preferred_element_type=jnp.float32)
    up_pre = jnp.dot(group_normed, mat_up, preferred_element_type=jnp.float32)
    sigma = jax.nn.sigmoid(gate_pre)
    silu_val = gate_pre * sigma
    hidden = (silu_val * up_pre).astype(jnp.bfloat16)
    hidden_all = lax.all_gather(hidden, "dp", axis=1, tiled=True)
    down_cols = jnp.dot(hidden_all, mat_down, preferred_element_type=jnp.float32)
    down_rows = lax.all_to_all(
        down_cols.astype(jnp.bfloat16), "dp", split_axis=0, concat_axis=1, tiled=True
    )
    output = (resid + down_rows.astype(jnp.float32)).astype(jnp.bfloat16)
    grad_resid = grad_low.astype(jnp.float32)
    grad_down = jnp.einsum("tf,td->fd", hidden_all, cot_cols, preferred_element_type=jnp.float32)
    grad_gate_pre = (grad_hidden * up_pre * sigma * (1.0 + gate_pre * (1.0 - sigma))).astype(
        jnp.bfloat16
    )
    grad_up_pre = (grad_hidden * silu_val).astype(jnp.bfloat16)
    grad_gate = jnp.einsum(
        "td,tf->df", group_normed, grad_gate_pre, preferred_element_type=jnp.float32
    )
    grad_up = jnp.einsum(
        "td,tf->df", group_normed, grad_up_pre, preferred_element_type=jnp.float32
    )
    grad_nm = jnp.einsum("tf,df->td", grad_gate_pre, mat_gate, preferred_element_type=jnp.float32)
    grad_nm = grad_nm + jnp.einsum(
        "tf,df->td", grad_up_pre, mat_up, preferred_element_type=jnp.float32
    )
    grad_nm = lax.psum_scatter(
        grad_nm.astype(jnp.bfloat16), "dp", scatter_dimension=0, tiled=True
    ).astype(jnp.float32)
    grad_gain_two = jnp.sum(grad_nm * resid * inv_two, axis=0)
    grad_resid = grad_resid + norm_back(resid, inv_two, gain_two, grad_nm)
    grad_branch = grad_resid.astype(jnp.bfloat16)
    grad_wo = jnp.einsum("tq,td->qd", att_low, grad_branch, preferred_element_type=jnp.float32)
    grad_att = jnp.einsum(
        "td,qd->tq", grad_branch, mat_out, preferred_element_type=jnp.float32
    ).astype(jnp.bfloat16)
    delta_all = delta_of(grad_att.reshape(tok_count, heads_kv, group_size, HEAD_SIZE), attended_set)
    back_keys_now = key_all
    back_values_now = value_all
    rows = query_vectors.shape[0]
    back_query_set = query_vectors.reshape(rows, heads_kv, group_size, HEAD_SIZE)
    grad_set = grad_att.reshape(rows, heads_kv, group_size, HEAD_SIZE)
    back_row_lab = piece_ids(query_pos, seq_starts)
    back_reach = reach_of(query_pos)

    def back_step(running, block_index):

        def back_live(dq_acc):
            key_piece = key_block(back_keys_now, block_index)
            value_piece = key_block(back_values_now, block_index)
            masked = scores_at(block_index, key_piece, back_query_set, query_pos, back_row_lab)
            chances = jnp.exp(masked - log_norm[..., None])
            upstream = jnp.einsum(
                "qhgd,khd->hgqk", grad_set, value_piece, preferred_element_type=jnp.float32
            )
            score_grad = (chances * (upstream - delta_all[..., None])).astype(jnp.bfloat16)
            key_grad = score_scale * jnp.einsum(
                "hgqk,qhgd->khd", score_grad, back_query_set, preferred_element_type=jnp.float32
            )
            value_grad = jnp.einsum(
                "hgqk,qhgd->khd",
                chances.astype(jnp.bfloat16),
                grad_set,
                preferred_element_type=jnp.float32,
            )
            dq_new = dq_acc + score_scale * jnp.einsum(
                "hgqk,khd->qhgd", score_grad, key_piece, preferred_element_type=jnp.float32
            )
            return dq_new, (key_grad.astype(jnp.bfloat16), value_grad.astype(jnp.bfloat16))

        none_grad = jnp.zeros((span, heads_kv, HEAD_SIZE), jnp.bfloat16)
        return lax.cond(
            block_index * span <= back_reach,
            back_live,
            lambda dq_acc: (dq_acc, (none_grad, none_grad)),
            running,
        )

    dq_set, kv_parts = lax.scan(
        back_step,
        jnp.zeros((rows, heads_kv, group_size, HEAD_SIZE), jnp.float32),
        jnp.arange(n_blocks),
    )
    dq_low = (
        rotary_back(dq_set.reshape(rows, -1, HEAD_SIZE), query_pos)
        .reshape(rows, -1)
        .astype(jnp.bfloat16)
    )
    kv_parts = jnp.concatenate([part.reshape(length, -1) for part in kv_parts], axis=1)
    kv_sums = lax.psum_scatter(kv_parts, "ctx", scatter_dimension=0, tiled=True).astype(jnp.float32)
    key_grads = kv_sums[:, : heads_kv * HEAD_SIZE].reshape(tok_count, heads_kv, HEAD_SIZE)
    value_grads = kv_sums[:, heads_kv * HEAD_SIZE :]
    dk_low = rotary_back(key_grads, query_pos).reshape(tok_count, -1).astype(jnp.bfloat16)
    dv_low = value_grads.reshape(tok_count, -1).astype(jnp.bfloat16)
    grad_wq = jnp.einsum("td,tq->dq", attention_normed, dq_low, preferred_element_type=jnp.float32)
    grad_wk = jnp.einsum("td,tq->dq", attention_normed, dk_low, preferred_element_type=jnp.float32)
    grad_wv = jnp.einsum("td,tq->dq", attention_normed, dv_low, preferred_element_type=jnp.float32)
    grad_na = jnp.einsum("tq,dq->td", dq_low, mat_query, preferred_element_type=jnp.float32)
    grad_na = grad_na + jnp.einsum(
        "tq,dq->td", dk_low, key_projection, preferred_element_type=jnp.float32
    )
    grad_na = grad_na + jnp.einsum(
        "tq,dq->td", dv_low, value_projection, preferred_element_type=jnp.float32
    )
    grad_gain_one = jnp.sum(grad_na * stream * inv_one, axis=0)
    input_grad = grad_resid + norm_back(stream, inv_one, gain_one, grad_na)
    n_dp = lax.axis_size("dp")
    n_ctx = lax.axis_size("ctx")
    cut = jnp.concatenate(
        [
            jnp.transpose(
                part.astype(jnp.bfloat16).reshape(part.shape[0], n_dp, -1), (1, 0, 2)
            )
            for part in (grad_wq, grad_wk, grad_wv, grad_wo)
        ],
        axis=2,
    )
    mine = lax.psum_scatter(
        cut.reshape(-1, cut.shape[2]), ("dp", "ctx"), scatter_dimension=0, tiled=True
    ).astype(jnp.float32)
    gate_up_sum = lax.psum_scatter(
        jnp.concatenate([grad_gate, grad_up], axis=1).astype(jnp.bfloat16),
        "ctx",
        scatter_dimension=0,
        tiled=True,
    ).astype(jnp.float32)
    down_sum = lax.psum_scatter(
        grad_down.astype(jnp.bfloat16), "ctx", scatter_dimension=0, tiled=True
    ).astype(jnp.float32)
    ff = w_gate.shape[1]
    e_one = w_query.shape[1]
    e_two = e_one + w_key.shape[1]
    e_three = e_two + w_value.shape[1]
    shards = (
        mine[:, :e_one],
        mine[:, e_one:e_two],
        mine[:, e_two:e_three],
        mine[:, e_three:],
        gate_up_sum[:, :ff],
        gate_up_sum[:, ff:],
        down_sum,
    )
    gain_both = lax.psum(jnp.stack([grad_gain_one, grad_gain_two]), ("dp", "ctx"))
    gain_rows = gain_attn.shape[0]
    gain_sums = lax.dynamic_slice_in_dim(
        gain_both, lax.axis_index("ctx") * gain_rows, gain_rows, 1
    )
    return (
        output[None],
        input_grad[None],
        gain_sums[0],
        gain_sums[1],
        shards[0],
        shards[1],
        shards[2],
        shards[3],
        shards[4],
        shards[5],
        shards[6],
    )


BF = jnp.bfloat16
F32 = jnp.float32
MESH = pl.DeviceIdType.MESH


def dot_nn(left, right):
    return lax.dot_general(left, right, (((1,), (0,)), ((), ())), preferred_element_type=F32)


def dot_nt(left, right):
    return lax.dot_general(left, right, (((1,), (1,)), ((), ())), preferred_element_type=F32)


def shift_lanes(field, amount):
    return pltpu.roll(field, amount, 1)


def widen(field, lanes):
    return jnp.concatenate(
        [field, jnp.zeros((field.shape[0], lanes - field.shape[1]), field.dtype)], axis=1
    )


def fast_kernel(
    n_dp,
    n_ctx,
    tok,
    cot,
    starts,
    gains,
    cos_ref,
    sin_ref,
    w_pack,
    w_gate,
    w_up,
    w_down,
    out_ref,
    ig_ref,
    gg_ref,
    g_pack_ref,
    g_gu_ref,
    g_down_ref,
    gb,
    wt,
    big,
    wd,
    wdz,
    na_ref,
    qt,
    kvb,
    sc,
    pp,
    rl,
    at,
    resid_ref,
    xb,
    cb,
    op,
    orecv,
    dn,
    drecv,
    dna,
    hb,
    dgu,
    xt,
    ct,
    gres,
    dat,
    rb,
    dkv,
    dkv_r,
    dkv_z,
    kvsum,
    gu_r,
    gu_z,
    gd,
    gd_r,
    gd_p,
    gd_z,
    g_r,
    g_p,
    g_z,
    nat,
    ggs,
    gg_p,
    gg_c,
    s_send,
    s_gain,
    s_a,
    s_ap,
    s_b,
    s_bz,
    s_bp,
    s_kv,
    s_gu,
    s_wd,
    s_wdz,
    s_x,
    s_c,
    s_o,
    s_d,
    s_dkv,
    s_gur,
    s_gdr,
    s_gdp,
    s_gdz,
    s_gr,
    s_gp,
    s_gz,
    s_ggp,
    s_ggc,
):
    n_z = n_ctx // 2
    rows_tok, model = tok.shape
    shard_rows = w_pack.shape[0]
    cq = model // n_dp
    ck = 96
    ffs = w_gate.shape[1]
    rf = w_down.shape[1]
    kvh = 6
    group = 3
    hs = HEAD_SIZE
    gl = group * rows_tok
    pack = w_pack.shape[1]
    d = lax.axis_index("dp")
    c = lax.axis_index("ctx")
    k = lax.rem(c, 2)
    z = c // 2
    mate = c + 1 - 2 * k
    my_down = pl.multiple_of(k * rf, 128)
    its_down = pl.multiple_of((1 - k) * rf, 128)
    big_sends = []
    pending = []
    counter = [0]

    def zc(i):
        return 2 * lax.rem(z + i, n_z) + k

    def dd_of(i):
        return lax.rem(d + i, n_dp)

    def rdma(src, dst, rsem, to_d, to_c, when=None):
        ssem = s_send.at[counter[0]]
        counter[0] += 1
        copy = pltpu.make_async_remote_copy(
            src_ref=src,
            dst_ref=dst,
            send_sem=ssem,
            recv_sem=rsem,
            device_id=(to_d, to_c),
            device_id_type=MESH,
        )
        if when is None:
            copy.start()
        else:
            pl.when(when)(copy.start)
        pending.append((copy, when))
        return pending[-1]

    def sent(entry):
        copy, when = entry
        if when is None:
            copy.wait_send()
        else:
            pl.when(when)(copy.wait_send)

    def arrived(dst, rsem):
        pltpu.make_async_remote_copy(
            src_ref=dst,
            dst_ref=dst,
            send_sem=s_send.at[0],
            recv_sem=rsem,
            device_id=(d, mate),
            device_id_type=MESH,
        ).wait_recv()

    middle = (z == 1) | (z == 2)
    hop = {1: z != n_z - 1, 2: None, 3: z != 0}

    def z_spread(ref, sem):
        return [
            rdma(ref(z), ref(z), sem(n_z - i), d, zc(i), when=hop[i]) for i in (2, 1, 3)
        ]

    def z_relay(ref, sem):
        e = lax.rem(z + 2, n_z)
        to = lax.rem(3 * (z + 3), n_z)
        arrived(ref(e), sem(2))
        return rdma(
            ref(e), ref(e), sem(lax.rem(e + n_z - to, n_z)), d, 2 * to + k, when=middle
        )

    def z_reduce(part, slot, sem):
        edge = (z == 0) | (z == n_z - 1)
        to = 1 + z // 3
        rdma(part(n_z - 1 - z), slot(n_z - 1), sem(n_z - 1), d, 2 * to + k, when=edge)
        for i in (1, 3):
            there = n_z - i - 1
            rdma(
                part(lax.rem(z + i, n_z)), slot(there), sem(there), d, zc(i), when=hop[i]
            )

    def z_reduce_rest(part, slot, sem):
        far = part(lax.rem(z + 2, n_z))

        @pl.when(middle)
        def _():
            arrived(slot(n_z - 1), sem(n_z - 1))
            far[...] = (far[...].astype(F32) + slot(n_z - 1)[...].astype(F32)).astype(BF)

        rdma(far, slot(1), sem(1), d, zc(2))

    def z_collect(total, slot, sem):
        arrived(slot(1), sem(1))
        total[...] += slot(1)[...].astype(F32)
        for j, there in ((0, z != n_z - 1), (2, z != 0)):

            @pl.when(there)
            def _():
                arrived(slot(j), sem(j))
                total[...] += slot(j)[...].astype(F32)

    def wa(e):
        return wt.at[d, e, k, :, la]

    def wb(e):
        return wt.at[d, e, k, :, lb]

    def row_half(e):
        return (lambda j: big.at[k, e, j]), (lambda j: s_gu.at[e, j])

    wt[d, z, k] = w_pack[...]
    gb[c] = gains[...]
    la = pl.ds(0, 512)
    lb = pl.ds(512, pack - 512)
    z_spread(wa, lambda j: s_a.at[0, j])
    for i in range(1, n_dp):
        rdma(wt.at[d, z, k, :, la], wt.at[d, z, k, :, la], s_a.at[n_dp - i, 0], dd_of(i), c)
    for i in range(1, n_ctx):
        rdma(gb.at[c], gb.at[c], s_gain.at[n_ctx - i], d, lax.rem(c + i, n_ctx))
    big[k, 0, z] = w_gate[...]
    big[k, 1, z] = w_up[...]
    wdz[z] = w_down[...]
    own = n_dp - 1
    cb[own] = cot[...]

    def down_rows(e):
        return pl.ds(pl.multiple_of(e * cq, 32), cq)

    z_spread(wb, lambda j: s_bz.at[j])
    z_spread(lambda j: wdz.at[j], lambda j: s_wdz.at[j])
    big_sends.extend(z_spread(*row_half(0)))
    stream = tok[...].astype(F32)
    inv1 = lax.rsqrt(jnp.mean(stream * stream, axis=1, keepdims=True) + norm_eps)

    z_relay(wa, lambda j: s_a.at[0, j])
    for q in (2, 1, 3):
        zq = lax.rem(z + q, n_z)
        if q != 2:
            arrived(wt.at[d, zq, k, :, la], s_a.at[0, q])
        for i in range(1, n_dp):
            rdma(
                wt.at[d, zq, k, :, la], wt.at[d, zq, k, :, la], s_a.at[n_dp - i, q], dd_of(i), c
            )
    rdma(wt.at[d, :, k, :, la], wt.at[d, :, k, :, la], s_ap.at[0], d, mate)
    z_relay(wb, lambda j: s_bz.at[j])
    z_relay(lambda j: wdz.at[j], lambda j: s_wdz.at[j])
    for r in range(1, n_dp):
        dr = dd_of(r)
        for q in range(n_z):
            arrived(wt.at[dr, lax.rem(z + q, n_z), k, :, la], s_a.at[r, q])
        rdma(wt.at[dr, :, k, :, la], wt.at[dr, :, k, :, la], s_ap.at[r], d, mate)

    gain_all = jnp.zeros((8, model), F32)
    for i in range(1, n_ctx):
        arrived(gb.at[lax.rem(c + i, n_ctx)], s_gain.at[i])
    for e in range(n_ctx):
        piece = widen(gb[e], model)
        gain_all = gain_all + (piece if e == 0 else shift_lanes(piece, shard_rows * e))
    gain1 = gain_all[0:1]
    gain2 = gain_all[1:2]
    normed = (stream * inv1 * gain1).astype(BF)
    na_ref[...] = normed

    kt = kvsum
    for r in range(n_dp):
        arrived(wt.at[dd_of(r), :, 1 - k, :, la], s_ap.at[r])

    def project(e, _):
        w = wt[e, :, :, :, 0:512].reshape(model, 512)
        o = dot_nn(na_ref[...], w)
        o_t = jnp.transpose(o)
        at[pl.ds(pl.multiple_of(e * cq, 32), cq), :] = o_t[:cq]
        kt[pl.ds(pl.multiple_of(e * ck, 32), ck), :] = o_t[cq : cq + ck]
        kt[pl.ds(pl.multiple_of(model // 3 + e * ck, 32), ck), :] = o_t[cq + ck : cq + 2 * ck]
        return 0

    big_sends.append(z_relay(*row_half(0)))
    lax.fori_loop(0, n_dp, project, 0)
    cosine = cos_ref[...]
    sine = sin_ref[...]
    half = hs // 2

    def turn(first, second):
        return first * cosine - second * sine, second * cosine + first * sine

    def turn_back(first, second):
        return first * cosine + second * sine, second * cosine - first * sine

    kvw = model // 3
    for g in range(kvh):
        lo, hi = turn(kt[g * hs : g * hs + half], kt[g * hs + half : (g + 1) * hs])
        kvb[c, 128 * g : 128 * g + 64, :] = jnp.concatenate([lo, hi], axis=0).astype(BF)
        kvb[c, 128 * g + 64 : 128 * g + 128, :] = kt[kvw + g * hs : kvw + (g + 1) * hs].astype(BF)
    def kv_of(j):
        return kvb.at[2 * j + k]

    z_spread(kv_of, lambda j: s_kv.at[j])
    rdma(kvb.at[c], kvb.at[c], s_kv.at[n_z], d, mate)
    big_sends.extend(z_spread(*row_half(1)))
    for h in range(kvh * group):
        lo, hi = turn(at[h * hs : h * hs + half], at[h * hs + half : (h + 1) * hs])
        low = jnp.concatenate([lo, hi], axis=0).astype(BF)
        qt[h * hs : (h + 1) * hs, :] = (low.astype(F32) * 0.125).astype(BF)

    for q in (1, 3):
        zq = lax.rem(z + q, n_z)
        arrived(wt.at[d, zq, k, :, lb], s_bz.at[q])
    for i in range(1, n_dp):
        rdma(wt.at[d, :, k, :, lb], wt.at[d, :, k, :, lb], s_b.at[n_dp - i], dd_of(i), c)
    rdma(wt.at[d, :, k, :, lb], wt.at[d, :, k, :, lb], s_bp.at[0], d, mate)
    for q in (1, 3):
        arrived(wdz.at[lax.rem(z + q, n_z)], s_wdz.at[q])
    for i in range(1, n_dp):
        e = dd_of(i)
        rdma(wdz.at[e], wd.at[down_rows(d), pl.ds(my_down, rf)], s_wd.at[n_dp - i], e, c)
    wd[down_rows(d), pl.ds(my_down, rf)] = wdz[d]
    for i in range(1, n_dp):
        rdma(cb.at[own], cb.at[n_dp - i - 1], s_c.at[n_dp - i - 1], dd_of(i), c)
    z_relay(kv_of, lambda j: s_kv.at[j])
    for q in (2, 1, 3):
        if q != 2:
            arrived(kvb.at[zc(q)], s_kv.at[q])
        rdma(kvb.at[zc(q)], kvb.at[zc(q)], s_kv.at[n_z + q], d, mate)
    for r in range(1, n_dp):
        dr = dd_of(r)
        arrived(wt.at[dr, :, k, :, lb], s_b.at[r])
        rdma(wt.at[dr, :, k, :, lb], wt.at[dr, :, k, :, lb], s_bp.at[r], d, mate)
    for q in range(n_z):
        arrived(kvb.at[2 * lax.rem(z + q, n_z) + 1 - k], s_kv.at[n_z + q])

    tpos = c * rows_tok + lax.broadcasted_iota(jnp.int32, (1, rows_tok), 1)
    lim = tpos
    for p in range(PICS):
        s_p = starts[0, p]
        lim = jnp.where((tpos >= s_p) & (tpos < s_p + PIC), jnp.maximum(lim, s_p + PIC - 1), lim)
    lim3 = jnp.concatenate([lim] * group, axis=1)

    def heads_of(ref, g):
        return jnp.concatenate(
            [
                ref[pl.ds(pl.multiple_of(g * group * hs + hs * j, hs), hs), :]
                for j in range(group)
            ],
            axis=1,
        )

    def attend(g, _):
        q_t = heads_of(qt, g)
        q_z = jnp.concatenate([q_t, jnp.zeros_like(q_t)], axis=0)
        k0 = pl.multiple_of(g * 128, 128)
        most = jnp.full((1, gl), -1e30, F32)
        for b in range(n_ctx):
            kv = jnp.transpose(kvb[b, pl.ds(k0, 128), :])
            s = dot_nn(kv, q_z)
            kpos = b * rows_tok + lax.broadcasted_iota(jnp.int32, (rows_tok, gl), 0)
            s = jnp.where(kpos <= lim3, s, -1e30)
            sc[b * rows_tok : (b + 1) * rows_tok, :] = s
            most = jnp.maximum(most, jnp.max(s, axis=0, keepdims=True))
        total = jnp.zeros((1, gl), F32)
        o_t = jnp.zeros((hs, gl), F32)
        for b in range(n_ctx):
            p = jnp.exp(sc[b * rows_tok : (b + 1) * rows_tok, :] - most)
            p_low = p.astype(BF)
            pp[g, b * rows_tok : (b + 1) * rows_tok, :] = p_low
            total = total + jnp.sum(p, axis=0, keepdims=True)
            o_t = o_t + dot_nn(kvb[b, pl.ds(pl.multiple_of(k0 + hs, hs), hs), :], p_low)
        inv = 1.0 / total
        rl[g] = jnp.broadcast_to(inv, (8, gl))
        o_t = o_t * inv
        for j in range(group):
            at[pl.ds(pl.multiple_of(g * group * hs + hs * j, hs), hs), :] = o_t[
                :, rows_tok * j : rows_tok * (j + 1)
            ]
        return 0

    lax.fori_loop(0, kvh, attend, 0)

    for r in range(1, n_dp):
        arrived(wd.at[down_rows(dd_of(r)), pl.ds(my_down, rf)], s_wd.at[r])
    rdma(wd.at[:, pl.ds(my_down, rf)], wd.at[:, pl.ds(my_down, rf)], s_wd.at[0], d, mate)
    big_sends.append(z_relay(*row_half(1)))
    for e in range(2):
        copy = rdma(big.at[k, e, z], big.at[k, e, z], s_gu.at[e, n_z], d, mate)
        big_sends.append(copy)
        for q in (2, 1, 3):
            zq = lax.rem(z + q, n_z)
            if q != 2:
                arrived(big.at[k, e, zq], s_gu.at[e, q])
            copy = rdma(big.at[k, e, zq], big.at[k, e, zq], s_gu.at[e, n_z + q], d, mate)
            big_sends.append(copy)

    att_t = at[...].astype(BF)
    nat[:, 0:rows_tok] = jnp.transpose(na_ref[...])
    nat[:, rows_tok : 2 * rows_tok] = att_t
    na_ref[...] = jnp.transpose(att_t)
    resid_ref[...] = tok[...].astype(F32)
    for r in range(n_dp):
        arrived(wt.at[dd_of(r), :, 1 - k, :, lb], s_bp.at[r])
    lead = 2 * ck + cq - 384

    def out_block(e, _):
        w = wt[e, :, :, :, 384:pack].reshape(model, pack - 384)
        o = dot_nn(na_ref[...], w)
        lane = lax.broadcasted_iota(jnp.int32, o.shape, 1)
        o = widen(jnp.where(lane >= lead, o, 0.0), model)
        resid_ref[...] += shift_lanes(o, lax.rem(e * cq + model - lead, model))
        return 0

    lax.fori_loop(0, n_dp, out_block, 0)
    resid = resid_ref[...]
    inv2 = lax.rsqrt(jnp.mean(resid * resid, axis=1, keepdims=True) + norm_eps)
    xb[own] = (resid * inv2 * gain2).astype(BF)
    for i in range(1, n_dp):
        rdma(xb.at[own], xb.at[n_dp - i - 1], s_x.at[n_dp - i - 1], dd_of(i), c)
    xt[:, own * rows_tok :] = jnp.transpose(xb[own])
    for p in range(n_dp - 1):
        arrived(cb.at[p], s_c.at[p])
    for p in range(n_dp):
        ct[:, p * rows_tok : (p + 1) * rows_tok] = jnp.transpose(cb[p])
    for e in range(2):
        for q in range(n_z):
            arrived(big.at[1 - k, e, lax.rem(z + q, n_z)], s_gu.at[e, n_z + q])
    arrived(wd.at[:, pl.ds(its_down, rf)], s_wd.at[0])
    for p in range(n_dp - 1):
        arrived(xb.at[p], s_x.at[p])

    nc = 256

    def weight_cols(e, n0):
        return jnp.concatenate(
            [big[b % 2, e, b // 2, :, pl.ds(n0, nc)] for b in range(n_ctx)], axis=0
        )

    for hf in range(n_dp // 2):
        t0 = 2 * hf
        r0 = t0 * rows_tok
        rh = 2 * rows_tok
        dna[...] = jnp.zeros_like(dna)

        def cols(n, _):
            n0 = pl.multiple_of(n * nc, nc)
            n1 = pl.multiple_of(n * nc + ffs, nc)
            x = xb[t0 : t0 + 2].reshape(rh, model)
            w_g = weight_cols(0, n0)
            w_u = weight_cols(1, n0)
            g = dot_nn(x, w_g)
            u = dot_nn(x, w_u)
            dh = dot_nn(cb[t0 : t0 + 2].reshape(rh, model), wd[:, pl.ds(n0, nc)])
            sg = jax.nn.sigmoid(g)
            si = g * sg
            hb[r0 : r0 + rh, pl.ds(n0, nc)] = (si * u).astype(BF)
            dg = (dh * u * sg * (1.0 + g * (1.0 - sg))).astype(BF)
            du = (dh * si).astype(BF)
            dgu[r0 : r0 + rh, pl.ds(n0, nc)] = dg
            dgu[r0 : r0 + rh, pl.ds(n1, nc)] = du
            dna[...] += dot_nt(dg, w_g) + dot_nt(du, w_u)
            return 0

        lax.fori_loop(0, ffs // nc, cols, 0)
        dn[t0 : t0 + 2] = dna[...].astype(BF).reshape(2, rows_tok, model)
        for p in (t0, t0 + 1):
            if p != own:
                there = n_dp - p - 2
                rdma(dn.at[p], drecv.at[there], s_d.at[there], dd_of(p + 1), c)
        y = dot_nt(hb[r0 : r0 + rh, :], wd[...])
        op[t0 : t0 + 2] = y.astype(BF).reshape(2, rows_tok, model)
        for p in (t0, t0 + 1):
            if p != own:
                there = n_dp - p - 2
                rdma(op.at[p], orecv.at[there], s_o.at[there], dd_of(p + 1), c)

    for p in range(n_dp - 1):
        xt[:, p * rows_tok : (p + 1) * rows_tok] = jnp.transpose(xb[p])
    for e in range(2):

        def gu_cols(n, _):
            n0 = pl.multiple_of(n * nc, nc)
            n1 = pl.multiple_of(n * nc + e * ffs, nc)
            r = dot_nn(xt[...], dgu[:, pl.ds(n1, nc)]).astype(BF)
            for b in range(n_ctx):
                big[b % 2, 2 + e, b // 2, :, pl.ds(n0, nc)] = r[
                    shard_rows * b : shard_rows * (b + 1)
                ]
            return 0

        lax.fori_loop(0, ffs // nc, gu_cols, 0)
    big_sends.append(rdma(big.at[1 - k, 2:4], gu_r, s_gur.at[0], d, mate))

    def gd_cols(j, _):
        r = dot_nn(ct[...], hb[:, pl.ds(pl.multiple_of(j * rf, 128), rf)]).astype(BF)
        for e in range(n_dp):
            gd[j, e] = r[cq * e : cq * (e + 1)]
        return 0

    lax.fori_loop(0, 2, gd_cols, 0)
    rdma(gd.at[1 - k], gd_r, s_gdr.at[0], d, mate)

    for p in range(n_dp - 1):
        arrived(drecv.at[p], s_d.at[p])
    d_nm = dna[rows_tok : 2 * rows_tok, :]
    for p in range(n_dp - 1):
        d_nm = d_nm + drecv[p].astype(F32)

    def norm_out(inputs, inverse, gain_vec, upstream):
        scaled = gain_vec * upstream
        return inverse * scaled - inputs * inverse * inverse * inverse * jnp.mean(
            scaled * inputs, axis=1, keepdims=True
        )

    resid = resid_ref[...]
    ggs[1:2, :] = jnp.sum(d_nm * resid * inv2, axis=0, keepdims=True)
    d_res = cot[...].astype(F32) + norm_out(resid, inv2, gain2, d_nm)
    gres[...] = d_res
    d_low = d_res.astype(BF).astype(F32)
    o0 = 2 * ck + cq
    for e in range(n_dp):
        t = shift_lanes(d_low, (o0 - cq * e) % model)[:, :pack]
        lane = lax.broadcasted_iota(jnp.int32, t.shape, 1)
        rb[e, rows_tok : 2 * rows_tok, :] = jnp.where(lane >= o0, t, 0.0).astype(BF)
    dna[...] = jnp.zeros_like(dna)

    def att_block(e, _):
        w = wt[e, :, :, :, 384:pack].reshape(model, pack - 384)
        dna[0:rows_tok, :] += dot_nt(rb[e, rows_tok : 2 * rows_tok, 384:pack], w)
        return 0

    lax.fori_loop(0, n_dp, att_block, 0)
    dat[...] = jnp.transpose(dna[0:rows_tok, :].astype(BF))

    arrived(gu_r, s_gur.at[0])

    def gu_sum(n, _):
        e = n // n_z
        j = lax.rem(n, n_z)
        gu_r[e, j] = (gu_r[e, j].astype(F32) + big[k, 2 + e, j].astype(F32)).astype(BF)
        return 0

    lax.fori_loop(0, 2 * n_z, gu_sum, 0)
    gu_set = (lambda j: gu_r.at[:, j], lambda j: gu_z.at[j], lambda j: s_gur.at[j + 1])
    z_reduce(*gu_set)
    arrived(gd_r, s_gdr.at[0])

    def gd_sum(e, _):
        gd_r[e] = (gd_r[e].astype(F32) + gd[k, e].astype(F32)).astype(BF)
        return 0

    lax.fori_loop(0, n_dp, gd_sum, 0)
    for i in range(1, n_dp):
        rdma(gd_r.at[dd_of(i)], gd_p.at[d], s_gdp.at[n_dp - i], dd_of(i), c)
    gd_p[d] = gd_r[d]

    for copy in big_sends:
        sent(copy)
    pending[:] = [copy for copy in pending if all(copy is not other for other in big_sends)]

    def store_pack(e, n0, t):
        for b in range(n_ctx):
            big[b % 2, e, b // 2, :, pl.ds(n0, nc)] = t[shard_rows * b : shard_rows * (b + 1)]

    def chip_sum(r, s, lanes):
        e = dd_of(r)
        arrived(g_r.at[e, :, :, lanes], s_gr.at[s, r])

        def one(j, _):
            mine = big[k, e, j, :, lanes].astype(F32)
            g_r[e, j, :, lanes] = (g_r[e, j, :, lanes].astype(F32) + mine).astype(BF)
            return 0

        lax.fori_loop(0, n_z, one, 0)
        return e

    def to_plane(s, lanes):
        for r in range(1, n_dp):
            e = chip_sum(r, s, lanes)
            there = n_dp - r - 1
            rdma(
                g_r.at[e, :, :, lanes], g_p.at[there, :, :, lanes], s_gp.at[s, there], e, c
            )

    def plane_sum(j, lanes):
        t = g_r[d, j, :, lanes].astype(F32)
        for p in range(n_dp - 1):
            t = t + g_p[p, j, :, lanes].astype(F32)
        return t

    def pack_set(s, lanes):
        return (
            lambda j: g_r.at[d, j, :, lanes],
            lambda j: g_z.at[j, :, lanes],
            lambda j: s_gz.at[s, j],
        )

    def to_z(s, lanes):
        for p in range(n_dp - 1):
            arrived(g_p.at[p, :, :, lanes], s_gp.at[s, p])
        for i in range(1, n_z):
            zq = lax.rem(z + i, n_z)
            g_r[d, zq, :, lanes] = plane_sum(zq, lanes).astype(BF)
        z_reduce(*pack_set(s, lanes))
        g_pack_ref[:, lanes] = plane_sum(z, lanes)

    def last_sum(s, lanes):
        z_collect(g_pack_ref.at[:, lanes], *pack_set(s, lanes)[1:])

    for r in (1, 2, 3, 0):
        e = dd_of(r)
        t = dot_nn(
            nat[:, rows_tok : 2 * rows_tok], rb[e, rows_tok : 2 * rows_tok, 512:pack]
        ).astype(BF)
        store_pack(e, 512, t)
        rdma(big.at[1 - k, e, :, :, lb], g_r.at[e, :, :, lb], s_gr.at[1, r], d, mate)
    to_plane(1, lb)
    z_reduce_rest(*gu_set)

    def attend_back(g, _):
        q_t = heads_of(qt, g)
        a_t = heads_of(dat, g)
        o_t = heads_of(at, g)
        none = jnp.zeros_like(q_t)
        inv = rl[g][0:1]
        delta = jnp.sum(a_t.astype(F32) * o_t, axis=0, keepdims=True) * inv
        a_z = jnp.concatenate([none, a_t], axis=0)
        a_inv = (a_t.astype(F32) * inv).astype(BF)
        q2 = jnp.transpose(jnp.concatenate([q_t, none], axis=0))
        a2 = jnp.transpose(jnp.concatenate([none, a_inv], axis=0))
        k0 = pl.multiple_of(g * 128, 128)
        dq = jnp.zeros((hs, gl), F32)
        for b in range(n_ctx):
            kv_t = kvb[b, pl.ds(k0, 128), :]
            dp = dot_nn(jnp.transpose(kv_t), a_z)
            p_low = pp[g, b * rows_tok : (b + 1) * rows_tok, :]
            ds = (p_low.astype(F32) * (dp * inv - delta)).astype(BF)
            dq = dq + dot_nn(kv_t[:hs], ds)
            both = dot_nn(ds, q2) + dot_nn(p_low, a2)
            dkv[b % 2, b // 2, pl.ds(k0, 128), :] = jnp.transpose(both).astype(BF)
        dq = dq * 0.125
        for j in range(group):
            at[pl.ds(pl.multiple_of(g * group * hs + hs * j, hs), hs), :] = dq[
                :, rows_tok * j : rows_tok * (j + 1)
            ]
        return 0

    lax.fori_loop(0, kvh, attend_back, 0)
    rdma(dkv.at[1 - k], dkv_r, s_dkv.at[0], d, mate)
    for h in range(kvh * group):
        lo, hi = turn_back(at[h * hs : h * hs + half], at[h * hs + half : (h + 1) * hs])
        qt[h * hs : (h + 1) * hs, :] = jnp.concatenate([lo, hi], axis=0).astype(BF)
    arrived(dkv_r, s_dkv.at[0])

    def kv_sum(j, _):
        dkv_r[j] = (dkv_r[j].astype(F32) + dkv[k, j].astype(F32)).astype(BF)
        return 0

    lax.fori_loop(0, n_z, kv_sum, 0)
    kv_set = (lambda j: dkv_r.at[j], lambda j: dkv_z.at[j], lambda j: s_dkv.at[j + 1])
    z_reduce(*kv_set)
    z_reduce_rest(*kv_set)
    chip_sum(0, 1, lb)
    to_z(1, lb)
    for r in range(1, n_dp):
        arrived(gd_p.at[dd_of(r)], s_gdp.at[r])
    gd_set = (lambda j: gd_p.at[j], lambda j: gd_z.at[j], lambda j: s_gdz.at[j])
    z_reduce(*gd_set)

    for p in range(n_dp - 1):
        arrived(orecv.at[p], s_o.at[p])
    y_all = resid_ref[...] + op[own].astype(F32)
    for p in range(n_dp - 1):
        y_all = y_all + orecv[p].astype(F32)
    out_ref[...] = y_all.astype(BF)

    kvsum[...] = dkv_r[z].astype(F32)
    z_collect(kvsum, *kv_set[1:])
    z_reduce_rest(*pack_set(1, lb))
    for g in range(kvh):
        r = 128 * g
        lo, hi = turn_back(kvsum[r : r + half], kvsum[r + half : r + hs])
        at[g * hs : (g + 1) * hs, :] = jnp.concatenate([lo, hi], axis=0)
        at[kvw + g * hs : kvw + (g + 1) * hs, :] = kvsum[r + hs : r + 2 * hs]
    for e in range(n_dp):
        rows = jnp.concatenate(
            [
                qt[cq * e : cq * (e + 1)],
                at[ck * e : ck * (e + 1)].astype(BF),
                at[kvw + ck * e : kvw + ck * (e + 1)].astype(BF),
                jnp.zeros((512 - o0, rows_tok), BF),
            ],
            axis=0,
        )
        rb[e, 0:rows_tok, :] = widen(jnp.transpose(rows), pack)

    for r in (1, 2, 3, 0):
        e = dd_of(r)

        def pack_cols(n, _):
            n0 = pl.multiple_of(n * nc, nc)
            store_pack(e, n0, dot_nn(nat[...], rb[e, :, pl.ds(n0, nc)]).astype(BF))
            return 0

        lax.fori_loop(0, 512 // nc, pack_cols, 0)
        rdma(big.at[1 - k, e, :, :, la], g_r.at[e, :, :, la], s_gr.at[0, r], d, mate)

    z_reduce_rest(*gd_set)
    to_plane(0, la)

    dna[...] = jnp.zeros_like(dna)

    def in_block(e, _):
        w = wt[e, :, :, :, 0:512].reshape(model, 512)
        dna[0:rows_tok, :] += dot_nt(rb[e, 0:rows_tok, 0:512], w)
        return 0

    lax.fori_loop(0, n_dp, in_block, 0)
    d_na = dna[0:rows_tok, :]
    stream = tok[...].astype(F32)
    ggs[0:1, :] = jnp.sum(d_na * stream * inv1, axis=0, keepdims=True)
    ig_ref[...] = gres[...] + norm_out(stream, inv1, gain1, d_na)
    for i in range(1, n_dp):
        there = n_dp - i - 1
        rdma(ggs, gg_p.at[there], s_ggp.at[there], dd_of(i), c)
    chip_sum(0, 0, la)
    for p in range(n_dp - 1):
        arrived(gg_p.at[p], s_ggp.at[p])
    gg_all = ggs[...]
    for p in range(n_dp - 1):
        gg_all = gg_all + gg_p[p]
    gg_c[0] = gg_all
    for i in range(1, n_ctx):
        rdma(gg_c.at[0], gg_c.at[n_ctx - i], s_ggc.at[n_ctx - i], d, lax.rem(c + i, n_ctx))
    g_gu_ref[...] = gu_r[:, z].astype(F32)
    z_collect(g_gu_ref, *gu_set[1:])
    g_down_ref[...] = gd_p[z].astype(F32)
    z_collect(g_down_ref, *gd_set[1:])
    last_sum(1, lb)
    to_z(0, la)
    z_reduce_rest(*pack_set(0, la))
    for i in range(1, n_ctx):
        arrived(gg_c.at[i], s_ggc.at[i])
    gg_tot = gg_c[0]
    for i in range(1, n_ctx):
        gg_tot = gg_tot + gg_c[i]
    gg_ref[...] = shift_lanes(gg_tot, lax.rem(model - shard_rows * c, model))[:, :256]
    last_sum(0, la)
    for copy in pending:
        sent(copy)
def fast_body(
    n_dp,
    n_ctx,
    tokens,
    starts,
    gain_attn,
    gain_mlp,
    w_query,
    w_key,
    w_value,
    w_out,
    w_gate,
    w_up,
    w_down,
    cotangent,
):
    n_z = n_ctx // 2
    rows_tok, model = tokens.shape[1:]
    sr = w_query.shape[0]
    rf, cd = w_down.shape
    ffs = w_gate.shape[1]
    cq = w_query.shape[1]
    ck = w_key.shape[1]
    pack = 2 * (cq + ck)
    length = rows_tok * n_ctx
    gl = 3 * rows_tok
    packed = jnp.concatenate([w_query, w_key, w_value, w_out], axis=1)
    down = jnp.transpose(w_down)
    gains = jnp.pad(
        jnp.stack([gain_attn, gain_mlp]).astype(jnp.float32), ((0, 6), (0, 256 - sr))
    )
    half = HEAD_SIZE // 2
    positions = lax.axis_index("ctx") * rows_tok + jnp.arange(rows_tok)
    freqs = 10000.0 ** (-jnp.arange(half).astype(jnp.float32) / half)
    angles = freqs[:, None] * positions.astype(jnp.float32)[None, :]
    vm = pl.BlockSpec(memory_space=pltpu.VMEM)
    dma = pltpu.SemaphoreType.DMA
    n = n_dp - 1
    scratch = [
        pltpu.VMEM((n_ctx, 8, 256), F32),
        pltpu.VMEM((n_dp, n_z, 2, sr, pack), BF),
        pltpu.VMEM((2, n_dp, n_z, sr, ffs), BF),
        pltpu.VMEM((model, 2 * rf), BF),
        pltpu.VMEM((n_z, cd, rf), BF),
        pltpu.VMEM((rows_tok, model), BF),
        pltpu.VMEM((model, rows_tok), BF),
        pltpu.VMEM((n_ctx, 2 * model // 3, rows_tok), BF),
        pltpu.VMEM((length, gl), F32),
        pltpu.VMEM((6, length, gl), BF),
        pltpu.VMEM((6, 8, gl), F32),
        pltpu.VMEM((model, rows_tok), F32),
        pltpu.VMEM((rows_tok, model), F32),
        pltpu.VMEM((n_dp, rows_tok, model), BF),
        pltpu.VMEM((n_dp, rows_tok, model), BF),
        pltpu.VMEM((n_dp, rows_tok, model), BF),
        pltpu.VMEM((n, rows_tok, model), BF),
        pltpu.VMEM((n_dp, rows_tok, model), BF),
        pltpu.VMEM((n, rows_tok, model), BF),
        pltpu.VMEM((2 * rows_tok, model), F32),
        pltpu.VMEM((n_dp * rows_tok, ffs), BF),
        pltpu.VMEM((n_dp * rows_tok, 2 * ffs), BF),
        pltpu.VMEM((model, n_dp * rows_tok), BF),
        pltpu.VMEM((model, n_dp * rows_tok), BF),
        pltpu.VMEM((rows_tok, model), F32),
        pltpu.VMEM((model, rows_tok), BF),
        pltpu.VMEM((n_dp, 2 * rows_tok, pack), BF),
        pltpu.VMEM((2, n_z, 2 * model // 3, rows_tok), BF),
        pltpu.VMEM((n_z, 2 * model // 3, rows_tok), BF),
        pltpu.VMEM((n_z, 2 * model // 3, rows_tok), BF),
        pltpu.VMEM((2 * model // 3, rows_tok), F32),
        pltpu.VMEM((2, n_z, sr, ffs), BF),
        pltpu.VMEM((n_z, 2, sr, ffs), BF),
        pltpu.VMEM((2, n_dp, cd, rf), BF),
        pltpu.VMEM((n_dp, cd, rf), BF),
        pltpu.VMEM((n_dp, cd, rf), BF),
        pltpu.VMEM((n_z, cd, rf), BF),
        pltpu.VMEM((n_dp, n_z, sr, pack), BF),
        pltpu.VMEM((n, n_z, sr, pack), BF),
        pltpu.VMEM((n_z, sr, pack), BF),
        pltpu.VMEM((model, 2 * rows_tok), BF),
        pltpu.VMEM((8, model), F32),
        pltpu.VMEM((n, 8, model), F32),
        pltpu.VMEM((n_ctx, 8, model), F32),
        dma((170,)),
        dma((n_ctx,)),
        dma((n_dp, n_z)),
        dma((n_dp,)),
        dma((n_dp,)),
        dma((n_z,)),
        dma((n_dp,)),
        dma((2 * n_z,)),
        dma((2, 2 * n_z)),
        dma((n_dp,)),
        dma((n_z,)),
        dma((n,)),
        dma((n,)),
        dma((n,)),
        dma((n,)),
        dma((n_z + 1,)),
        dma((n_z + 1,)),
        dma((1,)),
        dma((n_dp,)),
        dma((n_z,)),
        dma((2, n_dp)),
        dma((2, n)),
        dma((2, n_z)),
        dma((n,)),
        dma((n_ctx,)),
    ]
    out, ig, gg, g_pack, g_gu, g_down = pl.pallas_call(
        functools.partial(fast_kernel, n_dp, n_ctx),
        out_shape=(
            jax.ShapeDtypeStruct((rows_tok, model), BF),
            jax.ShapeDtypeStruct((rows_tok, model), F32),
            jax.ShapeDtypeStruct((8, 256), F32),
            jax.ShapeDtypeStruct((sr, pack), F32),
            jax.ShapeDtypeStruct((2, sr, ffs), F32),
            jax.ShapeDtypeStruct((cd, rf), F32),
        ),
        in_specs=[vm, vm, pl.BlockSpec(memory_space=pltpu.SMEM)] + [vm] * 7,
        out_specs=(vm,) * 6,
        scratch_shapes=scratch,
        compiler_params=pltpu.CompilerParams(
            has_side_effects=True, vmem_limit_bytes=67043328
        ),
        name="layer",
    )(
        tokens[0],
        cotangent[0],
        starts,
        gains,
        jnp.cos(angles),
        jnp.sin(angles),
        packed,
        w_gate,
        w_up,
        down,
    )
    return (
        out[None],
        ig[None],
        gg[0, :sr],
        gg[1, :sr],
        g_pack[:, :cq],
        g_pack[:, cq : cq + ck],
        g_pack[:, cq + ck : cq + 2 * ck],
        g_pack[:, cq + 2 * ck :],
        g_gu[0],
        g_gu[1],
        jnp.transpose(g_down),
    )


def solution(mesh):
    n_dp = mesh.shape["dp"]
    n_ctx = mesh.shape["ctx"]

    def choose(tokens, *rest):
        fits = n_dp == 4 and n_ctx == 2 * n_dp and tokens.shape[1:] == (128, 1152)
        if fits:
            return fast_body(n_dp, n_ctx, tokens, *rest)
        return body(tokens, *rest)

    return jax.shard_map(
        choose,
        mesh=mesh,
        in_specs=(
            P("dp", "ctx", None),
            P("dp", None),
            P("ctx"),
            P("ctx"),
            P("ctx", "dp"),
            P("ctx", "dp"),
            P("ctx", "dp"),
            P("ctx", "dp"),
            P("ctx", "dp"),
            P("ctx", "dp"),
            P("ctx", "dp"),
            P("dp", "ctx", None),
        ),
        out_specs=(
            P("dp", "ctx", None),
            P("dp", "ctx", None),
            P("ctx"),
            P("ctx"),
            P("ctx", "dp"),
            P("ctx", "dp"),
            P("ctx", "dp"),
            P("ctx", "dp"),
            P("ctx", "dp"),
            P("ctx", "dp"),
            P("ctx", "dp"),
        ),
        check_vma=False,
    )
```
